768 devices in a mesh: dom: 128 (over x, z_lo, y), band: 6 (over z_hi, core).
Axes of the slice: x: 4, y: 8, z: 12 (z_hi: 3, z_lo: 4; z = z_hi * 4 + z_lo), core: 2. Of those that a mesh axis runs over, the one named last changes fastest.
Arguments:
- wave: float32 [24, 512, 64, 128], P('band', 'dom'), parts along dimension 0, may hold values from -6 to 6
- potential: float32 [512, 64, 128], P('dom'), may hold values from -6 to 6
- energies: float32 [24], P('band'), parts along dimension 0, may hold values from -1 to 1
- proj_index: int32 [4096, 256], P('dom'), may hold values from 0 to 32767
- proj_values: float32 [4096, 8, 256], P('dom'), may hold values from -4 to 4
- slot_atom: int32 [4096], P('dom'), may hold values from 0 to 3072, as said below
- atom_rank: int32 [3072], replicated, may hold values from 0 to 3071, as said below
- d_matrix: float32 [3072, 8, 8], P('dom'), may hold values from -5 to 5
- q_matrix: float32 [3072, 8, 8], P('dom'), may hold values from -5 to 5
Outputs:
- residual: float32 [24, 512, 64, 128], P('band', 'dom'), parts along dimension 0
The draws below stay inside these ranges and needn't reach their ends.
There are 6 independent parts, one for each index of `band`. The reference program is written for one: setup_inputs(seed, part) draws one part's arguments, and reference() takes and returns one part's arrays. A program takes and returns all parts, laid end to end along the dimension named above; an argument that names none is the same for every part. Nothing has to cross between parts.
Inputs may be any that keep to these rules, and one draw needn't show every extreme that they name: `slot_atom`: every device holds at least 8 live slots, live slots come first among a device's slots, and in every draw some device has all 32 slots live and some has only 8. The atom of a live slot on device d has atom_rank // 24 within 2 of d, counted cyclically over the devices. `atom_rank`: A permutation of the atoms.
All inputs are finite; a program needn't handle non-finite values.
Results may differ from the reference program's by a relative error of at most 0.00007.
Values sent between devices are 32-bit elements; how exact they have to be, the bound alone decides.
No kernel may reach another device: no remote copies, remote signals or barrier semaphores. Data moves between devices by JAX's collectives and lax.ppermute only.
A program may use at most 64 MiB of HBM per device.

```python
import jax
import jax.numpy as jnp
from jax import lax

NB = 4
CX = 4
NY = 64
NZ = 128
NPROJ = 8
PTS = 256
SLOT_DEV = 32
ATOM_DEV = 24
NX = 512
SLOTS = 4096
ATOMS = 3072


def owner_order(key):
    return jax.random.permutation(jax.random.fold_in(key, 11), ATOMS).astype(jnp.int32)


def draw_atom_rank(key, part):
    return owner_order(key)


def draw_slot_atom(key, part):
    devices_count = SLOTS // SLOT_DEV
    ranking = owner_order(key)
    inverse = jnp.zeros((ATOMS,), jnp.int32).at[ranking].set(jnp.arange(ATOMS, dtype=jnp.int32))
    first, second, third, fourth, fifth = jax.random.split(jax.random.fold_in(key, 7), 5)
    counts = jax.random.randint(first, (devices_count,), SLOT_DEV // 4, SLOT_DEV + 1)
    full_dev = jax.random.randint(second, (), 0, devices_count)
    low_dev = (full_dev + 1 + jax.random.randint(third, (), 0, devices_count - 1)) % devices_count
    counts = counts.at[full_dev].set(SLOT_DEV).at[low_dev].set(SLOT_DEV // 4)
    within = jnp.arange(SLOTS) % SLOT_DEV
    device = jnp.arange(SLOTS) // SLOT_DEV
    offsets = jax.random.randint(fourth, (SLOTS,), -2, 3)
    owner = (device + offsets + devices_count) % devices_count
    place = owner * ATOM_DEV + jax.random.randint(fifth, (SLOTS,), 0, ATOM_DEV)
    atoms_drawn = inverse[place]
    return jnp.where(within < counts[device], atoms_drawn, ATOMS).astype(jnp.int32)


def with_ends(entries, own_key, least, largest):
    longest = entries.shape.index(max(entries.shape))
    spots = []
    for shift in (0, 1):
        where = [jax.random.randint(jax.random.fold_in(own_key, axis), (), 0, length) for axis, length in enumerate(entries.shape)]
        where[longest] = (where[longest] + shift) % entries.shape[longest]
        spots.append(tuple(where))
    return entries.at[spots[0]].set(least).at[spots[1]].set(largest)


def levels(rng, shape, cuts, least, largest):
    factor_of = 1.0
    for position, blocks in cuts:
        heights = jax.random.uniform(jax.random.fold_in(jax.random.fold_in(rng, 6), position), (blocks,), jnp.float32, least / len(cuts), largest / len(cuts))
        factor_of = factor_of * jnp.repeat(jnp.exp(heights), shape[position] // blocks).reshape((-1,) + (1,) * (len(shape) - 1 - position))
    return factor_of


def centred(key, shape, width, bound, cuts=(), kind=jnp.bfloat16):
    factor_of = levels(key, shape, cuts, -0.22, 0.18) if cuts else 1.0
    values = jax.random.normal(key, shape, jnp.float32) * width * factor_of
    return jnp.minimum(jnp.maximum(values, -bound), bound).astype(kind)


def setup_inputs(seed: int = 0, part: int = 0) -> dict:
    key_of = jax.random.split(jax.random.key(seed), 10)
    own_keys = jax.random.split(jax.random.fold_in(key_of[9], part), 10)
    return {
        "wave": centred(own_keys[0], (NB, NX, NY, NZ), 1.0, 6.0, ((1, 128),), jnp.float32),
        "potential": centred(key_of[1], (NX, NY, NZ), 1.0, 6.0, ((0, 128),), jnp.float32),
        "energies": jnp.clip(jax.random.uniform(own_keys[2], (NB,), jnp.float32, -1.0, 1.0), -1.0, 1.0),
        "proj_index": with_ends(jax.random.randint(key_of[3], (SLOTS, PTS), 0, CX * NY * NZ), jax.random.fold_in(key_of[3], 1), 0, (CX * NY * NZ) - 1).astype(jnp.int32),
        "proj_values": centred(key_of[4], (SLOTS, NPROJ, PTS), 0.25, 4.0, ((0, 128),), jnp.float32),
        "slot_atom": draw_slot_atom(jax.random.fold_in(key_of[9], 71), part),
        "atom_rank": draw_atom_rank(jax.random.fold_in(key_of[9], 71), part),
        "d_matrix": centred(key_of[7], (ATOMS, NPROJ, NPROJ), 0.35, 5.0, ((0, 128),), jnp.float32),
        "q_matrix": centred(key_of[8], (ATOMS, NPROJ, NPROJ), 0.35, 5.0, ((0, 128),), jnp.float32),
    }


HIGH = lax.Precision.HIGHEST


def laplace(field):
    total = jnp.zeros_like(field)
    for axis in (1, 2, 3):
        total = total - 2.5 * field
        total = total + (4.0 / 3.0) * (jnp.roll(field, 1, axis) + jnp.roll(field, -1, axis))
        total = total - (1.0 / 12.0) * (jnp.roll(field, 2, axis) + jnp.roll(field, -2, axis))
    return total


def reference(wave, potential, energies, proj_index, proj_values, slot_atom, atom_rank, d_matrix, q_matrix):
    bands = wave.shape[0]
    local = -0.5 * laplace(wave) + (potential[None] - energies[:, None, None, None]) * wave
    base = (jnp.arange(SLOTS) // SLOT_DEV * (CX * NY * NZ)).astype(jnp.int32)
    gidx = (proj_index + base[:, None]).astype(jnp.int32).reshape(-1)
    flat = wave.reshape(bands, -1)
    picked = flat[:, gidx].reshape(bands, SLOTS, PTS)
    coeff = jnp.einsum("nsp,sip->sni", picked, proj_values, precision=HIGH)
    live = slot_atom < ATOMS
    pos = jnp.where(live, atom_rank[jnp.minimum(slot_atom, ATOMS - 1)], ATOMS).astype(jnp.int32)
    total = jax.ops.segment_sum(coeff.reshape(SLOTS, -1), pos, num_segments=ATOMS + 1)[:ATOMS]
    total = total.reshape(ATOMS, bands, NPROJ)
    weight = jnp.einsum("aij,anj->ani", d_matrix, total, precision=HIGH)
    weight = weight - energies[None, :, None] * jnp.einsum("aij,anj->ani", q_matrix, total, precision=HIGH)
    padded = jnp.concatenate([weight, jnp.zeros((1, bands, NPROJ), jnp.float32)], axis=0)
    slot_weight = padded[pos]
    back = jnp.einsum("sni,sip->nsp", slot_weight, proj_values, precision=HIGH).reshape(bands, -1)
    result = local.reshape(bands, -1).at[:, gidx].add(back)
    return result.reshape(wave.shape)
```

```python
import functools

import jax
import jax.numpy as jnp
from jax import lax
from jax.experimental import pallas as pl
from jax.experimental.pallas import tpu as pltpu
from jax.sharding import PartitionSpec as P

HIGH = lax.Precision.HIGHEST
F32 = jnp.float32
BF16 = jnp.bfloat16
VMEM = pl.BlockSpec(memory_space=pltpu.VMEM)
SMEM = pl.BlockSpec(memory_space=pltpu.SMEM)
LANES = 128


def bf(x):
    return x.astype(F32).astype(BF16)


def gather_kernel(
    reach, n_dom, atoms_dev, me_ref, slot_ref, rank_ref, idx_ref, val_ref, wave_ref, out_ref, pos_ref, col_ref
):
    slots, points = idx_ref.shape
    nproj = val_ref.shape[1]
    bands, rows, _ = wave_ref.shape
    atoms_all = rank_ref.shape[0]
    kinds = bands * nproj
    halves = [slice(j, j + LANES) for j in range(0, points, LANES)]
    lane = lax.broadcasted_iota(jnp.int32, (kinds, LANES), 1)
    lane_row = lax.broadcasted_iota(jnp.int32, (8, LANES), 1)
    out_ref[...] = jnp.zeros_like(out_ref)
    me = me_ref[0]

    def body(s, carry):
        atom = slot_ref[s]
        live = atom < atoms_all
        pos = rank_ref[jnp.minimum(atom, atoms_all - 1)]
        owner = pos // atoms_dev
        off = owner - me + reach
        off = jnp.where(off < 0, off + n_dom, off)
        off = jnp.where(off >= n_dom, off - n_dom, off)
        column = jnp.where(live, off * atoms_dev + pos - owner * atoms_dev, -1).astype(F32)
        place = jnp.where(live, pos + 1, 0).astype(F32)
        pos_ref[pl.ds(s, 1), :] = jnp.full((1, LANES), place, F32)
        col_ref[pl.ds(s, 1), :] = jnp.full((1, LANES), column, F32)
        out_ref[kinds:, :] = jnp.where(lane_row == s, place, out_ref[kinds:, :])
        idx = jnp.broadcast_to(idx_ref[pl.ds(s, 1), :], (8, points))
        hb = idx >> 10
        hs = (idx >> 7) & 7
        lo = idx & 127
        accs = [[None] * len(halves) for _ in range(bands)]
        for k in range(rows // 8):
            hit = [hb[:, h] == k for h in halves]
            for n in range(bands):
                tbl = wave_ref[n, 8 * k : 8 * k + 8, :]
                for j, h in enumerate(halves):
                    g = jnp.take_along_axis(tbl, lo[:, h], axis=1, mode="promise_in_bounds")
                    accs[n][j] = g if k == 0 else jnp.where(hit[j], g, accs[n][j])
        cols = []
        for n in range(bands):
            total = None
            for j, h in enumerate(halves):
                pick = jnp.take_along_axis(accs[n][j], hs[:, h], axis=0, mode="promise_in_bounds")
                prod = pick * val_ref[s, :, h]
                total = prod if total is None else total + prod
            cols.append(jnp.sum(total, axis=1, keepdims=True))
        col = jnp.concatenate(cols, axis=0)
        out_ref[:kinds, :] = jnp.where(lane == s, col, out_ref[:kinds, :])
        return carry

    lax.fori_loop(0, slots, body, 0)


def local_kernel(energy_ref, wave_ref, low_ref, high_ref, pot_ref, out_ref):
    bands, planes, ny, nz = wave_ref.shape
    for n in range(bands):
        def plane(x):
            if x < 0:
                return low_ref[n, 2 + x]
            if x >= planes:
                return high_ref[n, x - planes]
            return wave_ref[n, x]

        for x in range(planes):
            f = wave_ref[n, x]
            near = plane(x - 1) + plane(x + 1)
            far = plane(x - 2) + plane(x + 2)
            near += pltpu.roll(f, 1, 0) + pltpu.roll(f, ny - 1, 0)
            near += pltpu.roll(f, 1, 1) + pltpu.roll(f, nz - 1, 1)
            far += pltpu.roll(f, 2, 0) + pltpu.roll(f, ny - 2, 0)
            far += pltpu.roll(f, 2, 1) + pltpu.roll(f, nz - 2, 1)
            scale = pot_ref[x] + (3.75 - energy_ref[n])
            out_ref[n, x] = scale * f - (2.0 / 3.0) * near + (1.0 / 24.0) * far


def scatter_kernel(
    chunk, energy_ref, own_ref, below_ref, above_ref, pos_ref, col_ref, dq_ref,
    idx_ref, val_ref, loc_ref, out_ref, a_ref, b_ref, acc_ref, w_ref
):
    slots, points = idx_ref.shape
    nproj = val_ref.shape[1]
    bands, rows, _ = loc_ref.shape
    kinds = bands * nproj
    total = None
    for ref in (own_ref, below_ref, above_ref):
        same = jnp.where(pos_ref[...] == ref[kinds : kinds + 1, :], 1.0, 0.0).astype(F32)
        part = lax.dot_general(
            ref[:kinds, :], same, (((1,), (1,)), ((), ())), precision=HIGH, preferred_element_type=F32
        )
        total = part if total is None else total + part
    window = dq_ref.shape[0]
    place = lax.broadcasted_iota(jnp.int32, (slots, LANES), 1).astype(F32)
    mine = jnp.where(col_ref[...] == place, 1.0, 0.0).astype(F32)[:, :window]
    picked = jnp.dot(mine, dq_ref[...], precision=HIGH, preferred_element_type=F32)
    matrices = picked.T
    square = nproj * nproj
    for n in range(bands):
        energy = energy_ref[n]
        mine_n = total[nproj * n : nproj * n + nproj]
        for i in range(nproj):
            at = nproj * i
            mixed = matrices[at : at + nproj] - energy * matrices[square + at : square + at + nproj]
            w_ref[nproj * n + i : nproj * n + i + 1, 0:slots] = jnp.sum(mixed * mine_n, axis=0, keepdims=True)

    lane = lax.broadcasted_iota(jnp.int32, (kinds, slots), 1)
    sub_lo = bf(lax.broadcasted_iota(jnp.int32, (LANES, points), 0))
    sub_hi = bf(lax.broadcasted_iota(jnp.int32, (rows, points), 0))
    zero = jnp.zeros((), BF16)
    one = jnp.ones((), BF16)
    piece = bands * LANES

    def build(s, base):
        idx = idx_ref[pl.ds(s, 1), :]
        lo = bf(idx & 127)
        hi = bf(idx >> 7)
        a_ref[:, base : base + points] = jnp.where(sub_hi == hi, one, zero)
        col = jnp.sum(jnp.where(lane == s, w_ref[:, 0:slots], 0.0), axis=1, keepdims=True)
        v = val_ref[s]
        hit = sub_lo == lo
        for n in range(bands):
            back = jnp.sum(col[nproj * n : nproj * n + nproj] * v, axis=0, keepdims=True)
            big = back.astype(BF16)
            small = (back - big.astype(F32)).astype(BF16)
            at = LANES * n
            b_ref[at : at + LANES, base : base + points] = jnp.where(hit, big, zero)
            b_ref[piece + at : piece + at + LANES, base : base + points] = jnp.where(hit, small, zero)

    acc_ref[...] = jnp.zeros_like(acc_ref)

    def body(c, carry):
        for j in range(chunk):
            build(c * chunk + j, points * j)
        acc_ref[...] += lax.dot_general(
            b_ref[...], a_ref[...], (((1,), (1,)), ((), ())), preferred_element_type=F32
        )
        return carry

    lax.fori_loop(0, slots // chunk, body, 0)
    for n in range(bands):
        at = LANES * n
        added = acc_ref[at : at + LANES] + acc_ref[piece + at : piece + at + LANES]
        out_ref[n] = loc_ref[n] + added.T


def shifted(value, axis, steps):
    count = lax.axis_size(axis)
    return lax.ppermute(value, axis, [(s, (s + steps) % count) for s in range(count)])


def per_device(
    wave, potential, energies, proj_index, proj_values, slot_atom, atom_rank, d_matrix, q_matrix
):
    bands, planes, ny, nz = wave.shape
    slots, points = proj_index.shape
    nproj = proj_values.shape[1]
    atoms_dev = d_matrix.shape[0]
    kinds = bands * nproj
    rows = planes * ny
    n_dom = lax.axis_size("dom")
    me = lax.axis_index("dom").astype(jnp.int32).reshape(1)
    reach = 2

    matrices = jnp.concatenate(
        [d_matrix.reshape(atoms_dev, -1), q_matrix.reshape(atoms_dev, -1)], axis=1
    )
    edge = bands * 2 * ny

    def halo(part):
        return jnp.concatenate([part.reshape(edge, nz), matrices], axis=0)

    from_low = shifted(halo(wave[:, planes - 2 :]), "dom", 1)
    from_high = shifted(halo(wave[:, :2]), "dom", -1)
    low = from_low[:edge].reshape(bands, 2, ny, nz)
    high = from_high[:edge].reshape(bands, 2, ny, nz)
    dq_low, dq_high = from_low[edge:], from_high[edge:]

    flat = wave.reshape(bands, rows, nz)
    mine, pos, col = pl.pallas_call(
        functools.partial(gather_kernel, reach, n_dom, atoms_dev),
        out_shape=(
            jax.ShapeDtypeStruct((kinds + 8, LANES), F32),
            jax.ShapeDtypeStruct((slots, LANES), F32),
            jax.ShapeDtypeStruct((slots, LANES), F32),
        ),
        in_specs=[SMEM, SMEM, SMEM, VMEM, VMEM, VMEM],
        out_specs=(VMEM, VMEM, VMEM),
        name="gather",
    )(me, slot_atom, atom_rank, proj_index, proj_values, flat)

    local = pl.pallas_call(
        local_kernel,
        out_shape=jax.ShapeDtypeStruct(wave.shape, F32),
        in_specs=[SMEM, VMEM, VMEM, VMEM, VMEM],
        out_specs=VMEM,
        name="local",
    )(energies, wave, low, high, potential)

    height = kinds + 8
    got_low = shifted(jnp.concatenate([mine, dq_low], axis=0), "dom", 1)
    got_high = shifted(jnp.concatenate([mine, dq_high], axis=0), "dom", -1)
    window = jnp.concatenate([got_low[height:], dq_low, matrices, dq_high, got_high[height:]], axis=0)
    triple = jnp.concatenate(
        [mine[:, :slots], got_low[:height, :slots], got_high[:height, :slots], jnp.zeros((height, LANES - 3 * slots), F32)],
        axis=1,
    )
    below = shifted(triple, "dom", 3)
    above = shifted(triple, "dom", -3)

    chunk = 4
    result = pl.pallas_call(
        functools.partial(scatter_kernel, chunk),
        out_shape=jax.ShapeDtypeStruct((bands, rows, nz), F32),
        in_specs=[SMEM] + [VMEM] * 9,
        out_specs=VMEM,
        scratch_shapes=[
            pltpu.VMEM((rows, points * chunk), BF16),
            pltpu.VMEM((2 * bands * LANES, points * chunk), BF16),
            pltpu.VMEM((2 * bands * LANES, rows), F32),
            pltpu.VMEM((kinds, LANES), F32),
        ],
        name="scatter",
    )(energies, triple, below, above, pos, col, window, proj_index, proj_values, local.reshape(bands, rows, nz))
    return result.reshape(wave.shape)


def solution(mesh):
    placed = (
        P("band", "dom", None, None),
        P("dom", None, None),
        P("band"),
        P("dom", None),
        P("dom", None, None),
        P("dom"),
        P(),
        P("dom", None, None),
        P("dom", None, None),
    )
    return jax.shard_map(
        per_device,
        mesh=mesh,
        in_specs=placed,
        out_specs=P("band", "dom", None, None),
        check_vma=False,
    )
```

```python
import functools

import jax
import jax.numpy as jnp
from jax import lax
from jax.experimental import pallas as pl
from jax.experimental.pallas import tpu as pltpu
from jax.sharding import PartitionSpec as P

HIGH = lax.Precision.HIGHEST
F32 = jnp.float32
BF16 = jnp.bfloat16
VMEM = pl.BlockSpec(memory_space=pltpu.VMEM)
SMEM = pl.BlockSpec(memory_space=pltpu.SMEM)
LANES = 128
HALF = 4
RING = 8
MIB = 1 << 20


def bf(x):
    return x.astype(F32).astype(BF16)


def pack_kernel(me_ref, d_ref, q_ref, wave_ref, inner_ref, outer_ref, sems):
    bands = wave_ref.shape[0]
    edge = wave_ref.shape[1] // 2
    even = (me_ref[0] & 1) == 0
    copies = []
    for index, (ref, upper) in enumerate(((inner_ref, even), (outer_ref, jnp.logical_not(even)))):
        start = pl.multiple_of(jnp.where(upper, edge, 0), edge)
        for n in range(bands):
            copy = pltpu.make_async_copy(
                wave_ref.at[n, pl.ds(start, edge), :],
                ref.at[pl.ds(n * edge, edge), :],
                sems.at[index, n],
            )
            copy.start()
            copies.append(copy)
    atoms_dev = d_ref.shape[1]
    matrices = jnp.concatenate([d_ref[...], q_ref[...]], axis=0)
    matrices = jnp.concatenate(
        [matrices, jnp.zeros((matrices.shape[0], LANES - atoms_dev), F32)], axis=1
    ).T[:atoms_dev]
    for ref in (inner_ref, outer_ref):
        ref[bands * edge :, :] = matrices
    for copy in copies:
        copy.wait()


def gather_kernel(
    chunk, n_dom, atoms_dev, me_ref, slot_ref, rank_ref, idx_ref, val_ref, wave_ref,
    out_ref, pos_ref, col_ref, grid_ref, hot_ref
):
    slots, points = idx_ref.shape
    nproj = val_ref.shape[1]
    bands, rows, _ = wave_ref.shape
    atoms_all = rank_ref.shape[0]
    kinds = bands * nproj
    halves = [slice(j, j + LANES) for j in range(0, points, LANES)]
    me = me_ref[0]
    first = (me & (HALF - 1)) * slots
    sign = jnp.where((me & 1) == 0, 1, -1)
    lane = lax.broadcasted_iota(jnp.int32, (kinds, LANES), 1) - first
    lane_row = lax.broadcasted_iota(jnp.int32, (8, LANES), 1) - first
    out_ref[...] = jnp.zeros_like(out_ref)
    for n in range(bands):
        w = wave_ref[n].T
        big = w.astype(BF16)
        grid_ref[LANES * n : LANES * n + LANES, :rows] = big
        grid_ref[LANES * n : LANES * n + LANES, rows:] = (w - big.astype(F32)).astype(BF16)
    sub_hi = bf(lax.broadcasted_iota(jnp.int32, (rows, points), 0))

    def body(c, carry):
        for j in range(chunk):
            idx = idx_ref[pl.ds(c * chunk + j, 1), :]
            hot = jnp.where(sub_hi == bf(idx >> 7), jnp.ones((), BF16), jnp.zeros((), BF16))
            hot_ref[:rows, points * j : points * j + points] = hot
            hot_ref[rows:, points * j : points * j + points] = hot
        lines = jnp.dot(grid_ref[...], hot_ref[...], preferred_element_type=F32)
        for j in range(chunk):
            s = c * chunk + j
            atom = slot_ref[s]
            live = atom < atoms_all
            pos = rank_ref[jnp.minimum(atom, atoms_all - 1)]
            owner = pos // atoms_dev
            off = (owner - me + n_dom // 2) & (n_dom - 1)
            off = (off - n_dom // 2) * sign
            block = jnp.where(off > 0, 2 * off - 1, -2 * off)
            column = jnp.where(live, block * atoms_dev + pos - owner * atoms_dev, -1).astype(F32)
            place = jnp.where(live, pos + 1, 0).astype(F32)
            pos_ref[pl.ds(s, 1), :] = jnp.full((1, LANES), place, F32)
            col_ref[pl.ds(s, 1), :] = jnp.full((1, LANES), column, F32)
            out_ref[kinds:, :] = jnp.where(lane_row == s, place, out_ref[kinds:, :])
            idx = jnp.broadcast_to(idx_ref[pl.ds(s, 1), :], (8, points))
            tile = (idx >> 3) & 15
            sub = idx & 7
            cols = []
            for n in range(bands):
                at = LANES * n
                acc = lines[at : at + 8, points * j : points * j + points]
                for k in range(1, LANES // 8):
                    acc = jnp.where(
                        tile == k, lines[at + 8 * k : at + 8 * k + 8, points * j : points * j + points], acc
                    )
                total = None
                for h in halves:
                    pick = jnp.take_along_axis(acc[:, h], sub[:, h], axis=0, mode="promise_in_bounds")
                    prod = pick * val_ref[s, :, h]
                    total = prod if total is None else total + prod
                cols.append(jnp.sum(total, axis=1, keepdims=True))
            col = jnp.concatenate(cols, axis=0)
            out_ref[:kinds, :] = jnp.where(lane == s, col, out_ref[:kinds, :])
        return carry

    lax.fori_loop(0, slots // chunk, body, 0)


def local_kernel(me_ref, energy_ref, wave_ref, inner_ref, outer_ref, pot_ref, out_ref):
    bands, planes, ny, nz = wave_ref.shape
    even = (me_ref[0] & 1) == 0

    def side(lower, n, p):
        at = (n * 2 + p) * ny
        inner = inner_ref[at : at + ny, :]
        outer = outer_ref[at : at + ny, :]
        return jnp.where(even, outer, inner) if lower else jnp.where(even, inner, outer)

    for n in range(bands):
        padded = [side(True, n, 0), side(True, n, 1)]
        padded += [wave_ref[n, x] for x in range(planes)]
        padded += [side(False, n, 0), side(False, n, 1)]
        for x in range(planes):
            f = padded[x + 2]
            near = padded[x + 1] + padded[x + 3]
            far = padded[x] + padded[x + 4]
            near += pltpu.roll(f, 1, 0) + pltpu.roll(f, ny - 1, 0)
            near += pltpu.roll(f, 1, 1) + pltpu.roll(f, nz - 1, 1)
            far += pltpu.roll(f, 2, 0) + pltpu.roll(f, ny - 2, 0)
            far += pltpu.roll(f, 2, 1) + pltpu.roll(f, nz - 2, 1)
            scale = pot_ref[x] + (3.75 - energy_ref[n])
            out_ref[n, x] = scale * f - (2.0 / 3.0) * near + (1.0 / 24.0) * far


def scatter_kernel(
    chunk, energy_ref, own_ref, below_ref, above_ref, pos_ref, col_ref, dq_ref,
    idx_ref, val_ref, loc_ref, out_ref, a_ref, b_ref, acc_ref, w_ref
):
    slots, points = idx_ref.shape
    nproj = val_ref.shape[1]
    bands, rows, _ = loc_ref.shape
    kinds = bands * nproj
    total = None
    for ref in (own_ref, below_ref, above_ref):
        same = jnp.where(pos_ref[...] == ref[kinds : kinds + 1, :], 1.0, 0.0).astype(F32)
        part = lax.dot_general(
            ref[:kinds, :], same, (((1,), (1,)), ((), ())), precision=HIGH, preferred_element_type=F32
        )
        total = part if total is None else total + part
    window = dq_ref.shape[0]
    place = lax.broadcasted_iota(jnp.int32, (slots, LANES), 1).astype(F32)
    mine = jnp.where(col_ref[...] == place, 1.0, 0.0).astype(F32)[:, :window]
    picked = jnp.dot(mine, dq_ref[...], precision=HIGH, preferred_element_type=F32)
    matrices = picked.T
    square = nproj * nproj
    for n in range(bands):
        energy = energy_ref[n]
        mine_n = total[nproj * n : nproj * n + nproj]
        for i in range(nproj):
            at = nproj * i
            mixed = matrices[at : at + nproj] - energy * matrices[square + at : square + at + nproj]
            w_ref[nproj * n + i : nproj * n + i + 1, 0:slots] = jnp.sum(mixed * mine_n, axis=0, keepdims=True)

    lane = lax.broadcasted_iota(jnp.int32, (kinds, slots), 1)
    sub_lo = bf(lax.broadcasted_iota(jnp.int32, (LANES, points), 0))
    sub_hi = bf(lax.broadcasted_iota(jnp.int32, (rows, points), 0))
    zero = jnp.zeros((), BF16)
    one = jnp.ones((), BF16)
    piece = bands * LANES

    def build(s, base):
        idx = idx_ref[pl.ds(s, 1), :]
        lo = bf(idx & 127)
        hi = bf(idx >> 7)
        a_ref[:, base : base + points] = jnp.where(sub_hi == hi, one, zero)
        col = jnp.sum(jnp.where(lane == s, w_ref[:, 0:slots], 0.0), axis=1, keepdims=True)
        v = val_ref[s]
        hit = sub_lo == lo
        for n in range(bands):
            back = jnp.sum(col[nproj * n : nproj * n + nproj] * v, axis=0, keepdims=True)
            big = back.astype(BF16)
            small = (back - big.astype(F32)).astype(BF16)
            at = LANES * n
            b_ref[at : at + LANES, base : base + points] = jnp.where(hit, big, zero)
            b_ref[piece + at : piece + at + LANES, base : base + points] = jnp.where(hit, small, zero)

    acc_ref[...] = jnp.zeros_like(acc_ref)

    def body(c, carry):
        for j in range(chunk):
            build(c * chunk + j, points * j)
        acc_ref[...] += lax.dot_general(
            b_ref[...], a_ref[...], (((1,), (1,)), ((), ())), preferred_element_type=F32
        )
        return carry

    lax.fori_loop(0, slots // chunk, body, 0)
    for n in range(bands):
        at = LANES * n
        added = acc_ref[at : at + LANES] + acc_ref[piece + at : piece + at + LANES]
        out_ref[n] = loc_ref[n] + added.T


def swapped(value, partner):
    count = lax.axis_size("dom")
    return lax.ppermute(value, "dom", [(s, partner(s) % count) for s in range(count)])


def inner_of(d):
    return d ^ 1


def outer_of(d):
    return d + 1 if d % 2 else d - 1


def second_of(d):
    return d ^ 2


def across_of(d):
    base, y = d - d % RING, d % RING
    return base + (6, 7, 4, 5, 2, 3, 0, 1)[y]


def beyond_of(d):
    base, y = d - d % RING, d % RING
    if y < HALF:
        return base - RING + (6, 7, 4, 5)[y]
    return base + RING + (2, 3, 0, 1)[y - HALF]


def per_device(
    wave, potential, energies, proj_index, proj_values, slot_atom, atom_rank, d_matrix, q_matrix
):
    bands, planes, ny, nz = wave.shape
    slots, points = proj_index.shape
    nproj = proj_values.shape[1]
    atoms_dev = d_matrix.shape[0]
    kinds = bands * nproj
    rows = planes * ny
    n_dom = lax.axis_size("dom")
    spot = lax.axis_index("dom").astype(jnp.int32)
    me = spot.reshape(1)
    flat = wave.reshape(bands, rows, nz)
    edge = bands * 2 * ny
    height = kinds + 8

    def turned(m):
        return jnp.transpose(m, (1, 2, 0)).reshape(nproj * nproj, atoms_dev)

    inner, outer = pl.pallas_call(
        pack_kernel,
        out_shape=(jax.ShapeDtypeStruct((edge + atoms_dev, nz), F32),) * 2,
        in_specs=[SMEM, VMEM, VMEM, pl.BlockSpec(memory_space=pl.ANY)],
        out_specs=(VMEM, VMEM),
        scratch_shapes=[pltpu.SemaphoreType.DMA((2, bands))],
        compiler_params=pltpu.CompilerParams(vmem_limit_bytes=4 * MIB),
        name="pack",
    )(me, turned(d_matrix), turned(q_matrix), flat)
    matrices = inner[edge:]
    outer_got = swapped(outer, outer_of)
    inner_got = swapped(inner, inner_of)

    chunk = 8
    mine, pos, col = pl.pallas_call(
        functools.partial(gather_kernel, chunk, n_dom, atoms_dev),
        out_shape=(
            jax.ShapeDtypeStruct((height, LANES), F32),
            jax.ShapeDtypeStruct((slots, LANES), F32),
            jax.ShapeDtypeStruct((slots, LANES), F32),
        ),
        in_specs=[SMEM, SMEM, SMEM, VMEM, VMEM, VMEM],
        out_specs=(VMEM, VMEM, VMEM),
        scratch_shapes=[
            pltpu.VMEM((bands * LANES, 2 * rows), BF16),
            pltpu.VMEM((2 * rows, points * chunk), BF16),
        ],
        compiler_params=pltpu.CompilerParams(vmem_limit_bytes=24 * MIB),
        cost_estimate=pl.CostEstimate(flops=10**10, bytes_accessed=10**7, transcendentals=0),
        name="gather",
    )(me, slot_atom, atom_rank, proj_index, proj_values, flat)

    def message(a, dq):
        return jnp.concatenate([a, dq], axis=0)

    outer_dq = outer_got[edge:]
    first = swapped(message(mine, outer_dq), inner_of)
    pair = mine + first[:height]
    second = swapped(message(pair, matrices), second_of)
    half = message(pair + second[:height], matrices)
    beyond = swapped(half, beyond_of)
    across = swapped(half, across_of)

    local = pl.pallas_call(
        local_kernel,
        out_shape=jax.ShapeDtypeStruct(wave.shape, F32),
        in_specs=[SMEM, SMEM, VMEM, VMEM, VMEM, VMEM],
        out_specs=VMEM,
        compiler_params=pltpu.CompilerParams(vmem_limit_bytes=8 * MIB),
        cost_estimate=pl.CostEstimate(flops=10**8, bytes_accessed=5 * 10**6, transcendentals=0),
        name="local",
    )(me, energies, wave, inner_got, outer_got, potential)

    y = spot % RING
    ends = (y == 0) | (y == RING - 1)
    middle = (y == HALF - 1) | (y == HALF)
    last = jnp.where(ends, beyond[height:], jnp.where(middle, across[height:], second[height:]))
    window = jnp.concatenate([matrices, inner_got[edge:], outer_dq, first[height:], last], axis=0)

    chunk = 4
    result = pl.pallas_call(
        functools.partial(scatter_kernel, chunk),
        out_shape=jax.ShapeDtypeStruct((bands, rows, nz), F32),
        in_specs=[SMEM] + [VMEM] * 9,
        out_specs=VMEM,
        scratch_shapes=[
            pltpu.VMEM((rows, points * chunk), BF16),
            pltpu.VMEM((2 * bands * LANES, points * chunk), BF16),
            pltpu.VMEM((2 * bands * LANES, rows), F32),
            pltpu.VMEM((kinds, LANES), F32),
        ],
        compiler_params=pltpu.CompilerParams(vmem_limit_bytes=24 * MIB),
        name="scatter",
    )(energies, half, beyond, across, pos, col, window, proj_index, proj_values, local.reshape(bands, rows, nz))
    return result.reshape(wave.shape)


def solution(mesh):
    placed = (
        P("band", "dom", None, None),
        P("dom", None, None),
        P("band"),
        P("dom", None),
        P("dom", None, None),
        P("dom"),
        P(),
        P("dom", None, None),
        P("dom", None, None),
    )
    return jax.shard_map(
        per_device,
        mesh=mesh,
        in_specs=placed,
        out_specs=P("band", "dom", None, None),
        check_vma=False,
    )
```

```python
import functools

import jax
import jax.numpy as jnp
from jax import lax
from jax.experimental import pallas as pl
from jax.experimental.pallas import tpu as pltpu
from jax.sharding import PartitionSpec as P

HIGH = lax.Precision.HIGHEST
F32 = jnp.float32
BF16 = jnp.bfloat16
VMEM = pl.BlockSpec(memory_space=pltpu.VMEM)
HBM = pl.BlockSpec(memory_space=pltpu.HBM)
SMEM = pl.BlockSpec(memory_space=pltpu.SMEM)
LANES = 128
HALF = 4
RING = 8
MIB = 1 << 20


def kept(x):
    return pltpu.with_memory_space_constraint(x, pltpu.HBM)


def bf(x):
    return x.astype(F32).astype(BF16)


def pack_kernel(me_ref, wave_ref, after_ref, inner_ref, outer_ref, sems):
    bands = wave_ref.shape[0]
    edge = wave_ref.shape[1] // 2
    even = (me_ref[0] & 1) == 0
    copies = []
    for index, (ref, upper) in enumerate(((inner_ref, even), (outer_ref, jnp.logical_not(even)))):
        start = pl.multiple_of(jnp.where(upper, edge, 0), edge)
        for n in range(bands):
            copy = pltpu.make_async_copy(
                wave_ref.at[n, pl.ds(start, edge), :],
                ref.at[pl.ds(n * edge, edge), :],
                sems.at[index, n],
            )
            copy.start()
            copies.append(copy)
    for copy in copies:
        copy.wait()


def gather_kernel(
    chunk, me_ref, slot_ref, rank_ref, idx_hbm, val_hbm, wave_hbm, d_hbm, q_hbm,
    out_ref, pos_ref, col_ref,
    idx_ref, val_ref, wave_ref, d_ref, q_ref, grid_ref, hot_ref, sems
):
    slots, points = idx_ref.shape
    nproj = val_ref.shape[1]
    bands, rows, _ = wave_ref.shape
    atoms_all = rank_ref.shape[0]
    atoms_dev = d_ref.shape[1]
    kinds = bands * nproj
    height = kinds + 8
    copies = [pltpu.make_async_copy(idx_hbm, idx_ref, sems.at[0])]
    copies += [pltpu.make_async_copy(wave_hbm.at[n], wave_ref.at[n], sems.at[1 + n]) for n in range(bands)]
    copies.append(pltpu.make_async_copy(val_hbm, val_ref, sems.at[1 + bands]))
    copies.append(pltpu.make_async_copy(d_hbm, d_ref, sems.at[2 + bands]))
    copies.append(pltpu.make_async_copy(q_hbm, q_ref, sems.at[3 + bands]))
    for copy in copies:
        copy.start()
    halves = [slice(j, j + LANES) for j in range(0, points, LANES)]
    me = me_ref[0]
    first = (me & (HALF - 1)) * slots
    lane = lax.broadcasted_iota(jnp.int32, (kinds, LANES), 1) - first
    lane_row = lax.broadcasted_iota(jnp.int32, (8, LANES), 1) - first
    out_ref[:height, :] = jnp.zeros((height, LANES), F32)
    pos_ref[...] = jnp.zeros_like(pos_ref)
    col_ref[...] = jnp.full_like(col_ref, -1.0)
    sub_hi = bf(lax.broadcasted_iota(jnp.int32, (rows, points), 0))
    for n in range(bands):
        copies[1 + n].wait()
        w = wave_ref[n].T
        big = w.astype(BF16)
        grid_ref[LANES * n : LANES * n + LANES, :rows] = big
        grid_ref[LANES * n : LANES * n + LANES, rows:] = (w - big.astype(F32)).astype(BF16)
    copies[0].wait()
    for copy in copies[1 + bands :]:
        copy.wait()
    matrices = jnp.concatenate([d_ref[...], q_ref[...]], axis=0)
    matrices = jnp.concatenate(
        [matrices, jnp.zeros((matrices.shape[0], LANES - atoms_dev), F32)], axis=1
    )
    out_ref[height:, :] = matrices.T[:atoms_dev]

    def body(c, carry):
        @pl.when(slot_ref[c * chunk] < atoms_all)
        def _():
            for j in range(chunk):
                idx = idx_ref[pl.ds(c * chunk + j, 1), :]
                hot = jnp.where(sub_hi == bf(idx >> 7), jnp.ones((), BF16), jnp.zeros((), BF16))
                hot_ref[:rows, points * j : points * j + points] = hot
                hot_ref[rows:, points * j : points * j + points] = hot
            lines = jnp.dot(grid_ref[...], hot_ref[...], preferred_element_type=F32)
            for j in range(chunk):
                s = c * chunk + j
                atom = slot_ref[s]
                live = atom < atoms_all
                pos = rank_ref[jnp.minimum(atom, atoms_all - 1)]
                owner = pos // atoms_dev
                apart = owner ^ me
                block = jnp.where(apart < RING, HALF, HALF + 2) + (apart & 1)
                block = jnp.where(apart < HALF, apart, block)
                column = jnp.where(live, block * atoms_dev + pos - owner * atoms_dev, -1).astype(F32)
                place = jnp.where(live, pos + 1, 0).astype(F32)
                pos_ref[pl.ds(s, 1), :] = jnp.full((1, LANES), place, F32)
                col_ref[pl.ds(s, 1), :] = jnp.full((1, LANES), column, F32)
                out_ref[kinds:height, :] = jnp.where(lane_row == s, place, out_ref[kinds:height, :])
                idx = jnp.broadcast_to(idx_ref[pl.ds(s, 1), :], (8, points))
                tile = (idx >> 3) & 15
                sub = idx & 7
                cols = []
                for n in range(bands):
                    at = LANES * n
                    acc = lines[at : at + 8, points * j : points * j + points]
                    for k in range(1, LANES // 8):
                        acc = jnp.where(
                            tile == k, lines[at + 8 * k : at + 8 * k + 8, points * j : points * j + points], acc
                        )
                    total = None
                    for h in halves:
                        pick = jnp.take_along_axis(acc[:, h], sub[:, h], axis=0, mode="promise_in_bounds")
                        prod = pick * val_ref[s, :, h]
                        total = prod if total is None else total + prod
                    cols.append(jnp.sum(total, axis=1, keepdims=True))
                col = jnp.concatenate(cols, axis=0)
                out_ref[:kinds, :] = jnp.where(lane == s, col, out_ref[:kinds, :])

        return carry

    lax.fori_loop(0, slots // chunk, body, 0)


def finish_kernel(me_ref, energy_ref, wave_ref, inner_ref, outer_ref, pot_ref, add_ref, out_hbm, out_ref, sems):
    bands, planes, ny, nz = wave_ref.shape
    even = (me_ref[0] & 1) == 0

    def side(lower, n, p):
        at = (n * 2 + p) * ny
        inner = inner_ref[at : at + ny, :]
        outer = outer_ref[at : at + ny, :]
        return jnp.where(even, outer, inner) if lower else jnp.where(even, inner, outer)

    copies = []
    for n in range(bands):
        padded = [side(True, n, 0), side(True, n, 1)]
        padded += [wave_ref[n, x] for x in range(planes)]
        padded += [side(False, n, 0), side(False, n, 1)]
        for x in range(planes):
            f = padded[x + 2]
            near = padded[x + 1] + padded[x + 3]
            far = padded[x] + padded[x + 4]
            near += pltpu.roll(f, 1, 0) + pltpu.roll(f, ny - 1, 0)
            near += pltpu.roll(f, 1, 1) + pltpu.roll(f, nz - 1, 1)
            far += pltpu.roll(f, 2, 0) + pltpu.roll(f, ny - 2, 0)
            far += pltpu.roll(f, 2, 1) + pltpu.roll(f, nz - 2, 1)
            scale = pot_ref[x] + (3.75 - energy_ref[n])
            added = add_ref[n, ny * x : ny * x + ny, :]
            out_ref[n, x] = added + (scale * f - (2.0 / 3.0) * near + (1.0 / 24.0) * far)
        copy = pltpu.make_async_copy(out_ref.at[n], out_hbm.at[n], sems.at[n])
        copy.start()
        copies.append(copy)
    for copy in copies:
        copy.wait()


def scatter_kernel(
    chunk, atoms_all, energy_ref, slot_ref, own_ref, second_ref, across_ref, beyond_ref,
    pos_ref, col_ref, idx_ref, val_ref, out_ref, a_ref, b_ref, acc_ref, w_ref
):
    slots, points = idx_ref.shape
    nproj = val_ref.shape[1]
    bands, rows, _ = out_ref.shape
    kinds = bands * nproj
    height = kinds + 8
    total = None
    for ref in (own_ref, across_ref, beyond_ref):
        same = jnp.where(pos_ref[...] == ref[kinds : kinds + 1, :], 1.0, 0.0).astype(F32)
        part = lax.dot_general(
            ref[:kinds, :], same, (((1,), (1,)), ((), ())), precision=HIGH, preferred_element_type=F32
        )
        total = part if total is None else total + part
    window = jnp.concatenate(
        [ref[height:, :] for ref in (own_ref, second_ref, across_ref, beyond_ref)], axis=0
    )
    place = lax.broadcasted_iota(jnp.int32, (slots, window.shape[0]), 1).astype(F32)
    mine = jnp.where(col_ref[:, :1] == place, 1.0, 0.0).astype(F32)
    picked = jnp.dot(mine, window, precision=HIGH, preferred_element_type=F32)
    matrices = picked.T
    square = nproj * nproj
    for n in range(bands):
        energy = energy_ref[n]
        mine_n = total[nproj * n : nproj * n + nproj]
        for i in range(nproj):
            at = nproj * i
            mixed = matrices[at : at + nproj] - energy * matrices[square + at : square + at + nproj]
            w_ref[nproj * n + i : nproj * n + i + 1, 0:slots] = jnp.sum(mixed * mine_n, axis=0, keepdims=True)

    lane = lax.broadcasted_iota(jnp.int32, (kinds, slots), 1)
    sub_lo = bf(lax.broadcasted_iota(jnp.int32, (LANES, points), 0))
    sub_hi = bf(lax.broadcasted_iota(jnp.int32, (rows, points), 0))
    zero = jnp.zeros((), BF16)
    one = jnp.ones((), BF16)
    piece = bands * LANES

    def build(s, base):
        idx = idx_ref[pl.ds(s, 1), :]
        lo = bf(idx & 127)
        hi = bf(idx >> 7)
        a_ref[:, base : base + points] = jnp.where(sub_hi == hi, one, zero)
        col = jnp.sum(jnp.where(lane == s, w_ref[:, 0:slots], 0.0), axis=1, keepdims=True)
        v = val_ref[s]
        hit = sub_lo == lo
        for n in range(bands):
            back = jnp.sum(col[nproj * n : nproj * n + nproj] * v, axis=0, keepdims=True)
            big = back.astype(BF16)
            small = (back - big.astype(F32)).astype(BF16)
            at = LANES * n
            b_ref[at : at + LANES, base : base + points] = jnp.where(hit, big, zero)
            b_ref[piece + at : piece + at + LANES, base : base + points] = jnp.where(hit, small, zero)

    acc_ref[...] = jnp.zeros_like(acc_ref)

    def body(c, carry):
        @pl.when(slot_ref[c * chunk] < atoms_all)
        def _():
            for j in range(chunk):
                build(c * chunk + j, points * j)
            acc_ref[...] += lax.dot_general(
                b_ref[...], a_ref[...], (((1,), (1,)), ((), ())), preferred_element_type=F32
            )

        return carry

    lax.fori_loop(0, slots // chunk, body, 0)
    for n in range(bands):
        at = LANES * n
        out_ref[n] = (acc_ref[at : at + LANES] + acc_ref[piece + at : piece + at + LANES]).T


def swapped(value, partner):
    count = lax.axis_size("dom")
    return lax.ppermute(value, "dom", [(s, partner(s) % count) for s in range(count)])


def inner_of(d):
    return d ^ 1


def outer_of(d):
    return d + 1 if d % 2 else d - 1


def second_of(d):
    return d ^ 2


def across_of(d):
    base, y = d - d % RING, d % RING
    return base + (6, 7, 4, 5, 2, 3, 0, 1)[y]


def beyond_of(d):
    base, y = d - d % RING, d % RING
    if y < HALF:
        return base - RING + (6, 7, 4, 5)[y]
    return base + RING + (2, 3, 0, 1)[y - HALF]


def per_device(
    wave, potential, energies, proj_index, proj_values, slot_atom, atom_rank, d_matrix, q_matrix
):
    bands, planes, ny, nz = wave.shape
    slots, points = proj_index.shape
    nproj = proj_values.shape[1]
    atoms_dev = d_matrix.shape[0]
    atoms_all = atom_rank.shape[0]
    kinds = bands * nproj
    rows = planes * ny
    me = lax.axis_index("dom").astype(jnp.int32).reshape(1)
    flat = wave.reshape(bands, rows, nz)
    edge = bands * 2 * ny
    height = kinds + 8
    square = nproj * nproj

    def turned(m):
        return jnp.transpose(m, (1, 2, 0)).reshape(square, atoms_dev)

    chunk = 8
    mine, pos, col = pl.pallas_call(
        functools.partial(gather_kernel, chunk),
        out_shape=(
            jax.ShapeDtypeStruct((height + atoms_dev, LANES), F32),
            jax.ShapeDtypeStruct((slots, LANES), F32),
            jax.ShapeDtypeStruct((slots, LANES), F32),
        ),
        in_specs=[SMEM, SMEM, SMEM, HBM, HBM, HBM, HBM, HBM],
        out_specs=(VMEM, VMEM, VMEM),
        scratch_shapes=[
            pltpu.VMEM(proj_index.shape, jnp.int32),
            pltpu.VMEM(proj_values.shape, F32),
            pltpu.VMEM(flat.shape, F32),
            pltpu.VMEM((square, atoms_dev), F32),
            pltpu.VMEM((square, atoms_dev), F32),
            pltpu.VMEM((bands * LANES, 2 * rows), BF16),
            pltpu.VMEM((2 * rows, points * chunk), BF16),
            pltpu.SemaphoreType.DMA((4 + bands,)),
        ],
        compiler_params=pltpu.CompilerParams(vmem_limit_bytes=24 * MIB),
        cost_estimate=pl.CostEstimate(flops=10**10, bytes_accessed=10**7, transcendentals=0),
        name="gather",
    )(me, kept(slot_atom), kept(atom_rank), kept(proj_index), kept(proj_values), kept(flat), kept(turned(d_matrix)), kept(turned(q_matrix)))

    first = swapped(mine, inner_of)
    pair = mine[:height] + first[:height]
    known = [mine[height:], first[height:]]
    second = swapped(jnp.concatenate([pair] + known, axis=0), second_of)
    half = jnp.concatenate([pair + second[:height]] + known, axis=0)

    inner, outer = pl.pallas_call(
        pack_kernel,
        out_shape=(jax.ShapeDtypeStruct((edge, nz), F32),) * 2,
        in_specs=[SMEM, HBM, pl.BlockSpec(memory_space=pl.ANY)],
        out_specs=(VMEM, VMEM),
        scratch_shapes=[pltpu.SemaphoreType.DMA((2, bands))],
        compiler_params=pltpu.CompilerParams(vmem_limit_bytes=4 * MIB),
        cost_estimate=pl.CostEstimate(flops=10**6, bytes_accessed=10**6, transcendentals=0),
        name="pack",
    )(me, kept(flat), col)
    half, inner, outer = lax.optimization_barrier((half, inner, outer))
    beyond = swapped(half, beyond_of)
    across = swapped(half, across_of)
    outer_got = swapped(outer, outer_of)
    inner_got = swapped(inner, inner_of)

    chunk = 4
    added = pl.pallas_call(
        functools.partial(scatter_kernel, chunk, atoms_all),
        out_shape=jax.ShapeDtypeStruct((bands, rows, nz), F32),
        in_specs=[SMEM, SMEM] + [VMEM] * 8,
        out_specs=VMEM,
        scratch_shapes=[
            pltpu.VMEM((rows, points * chunk), BF16),
            pltpu.VMEM((2 * bands * LANES, points * chunk), BF16),
            pltpu.VMEM((2 * bands * LANES, rows), F32),
            pltpu.VMEM((kinds, LANES), F32),
        ],
        compiler_params=pltpu.CompilerParams(vmem_limit_bytes=24 * MIB),
        cost_estimate=pl.CostEstimate(flops=10**10, bytes_accessed=10**7, transcendentals=0),
        name="scatter",
    )(kept(energies), kept(slot_atom), half, second, across, beyond, pos, col, proj_index, proj_values)

    return pl.pallas_call(
        finish_kernel,
        out_shape=jax.ShapeDtypeStruct(wave.shape, F32),
        in_specs=[SMEM, SMEM, VMEM, VMEM, VMEM, VMEM, VMEM],
        out_specs=HBM,
        scratch_shapes=[pltpu.VMEM(wave.shape, F32), pltpu.SemaphoreType.DMA((bands,))],
        compiler_params=pltpu.CompilerParams(vmem_limit_bytes=8 * MIB),
        name="finish",
    )(me, energies, wave, inner_got, outer_got, potential, added)


def solution(mesh):
    placed = (
        P("band", "dom", None, None),
        P("dom", None, None),
        P("band"),
        P("dom", None),
        P("dom", None, None),
        P("dom"),
        P(),
        P("dom", None, None),
        P("dom", None, None),
    )
    return jax.shard_map(
        per_device,
        mesh=mesh,
        in_specs=placed,
        out_specs=P("band", "dom", None, None),
        check_vma=False,
    )
```

```python
import functools

import jax
import jax.numpy as jnp
from jax import lax
from jax.experimental import pallas as pl
from jax.experimental.pallas import tpu as pltpu
from jax.sharding import PartitionSpec as P


HIGH = lax.Precision.HIGHEST
F32 = jnp.float32
BF16 = jnp.bfloat16
VMEM = pl.BlockSpec(memory_space=pltpu.VMEM)
HBM = pl.BlockSpec(memory_space=pltpu.HBM)
SMEM = pl.BlockSpec(memory_space=pltpu.SMEM)
LANES = 128
HALF = 4
RING = 8
MIB = 1 << 20


def kept(x):
    return pltpu.with_memory_space_constraint(x, pltpu.HBM)


def bf(x):
    return x.astype(F32).astype(BF16)


def pack_kernel(me_ref, wave_ref, after_ref, inner_ref, outer_ref, sems):
    bands = wave_ref.shape[0]
    edge = wave_ref.shape[1] // 2
    even = (me_ref[0] & 1) == 0
    copies = []
    for index, (ref, upper) in enumerate(((inner_ref, even), (outer_ref, jnp.logical_not(even)))):
        start = pl.multiple_of(jnp.where(upper, edge, 0), edge)
        for n in range(bands):
            copy = pltpu.make_async_copy(
                wave_ref.at[n, pl.ds(start, edge), :],
                ref.at[pl.ds(n * edge, edge), :],
                sems.at[index, n],
            )
            copy.start()
            copies.append(copy)
    for copy in copies:
        copy.wait()


def gather_kernel(
    chunk, aside, me_ref, slot_ref, rank_ref, idx_hbm, val_hbm, wave_hbm, d_hbm, q_hbm,
    out_ref, pos_ref, col_ref,
    idx_ref, val_ref, wave_ref, d_ref, q_ref, grid_ref, hot_ref, sems
):
    slots, points = idx_ref.shape
    nproj = val_ref.shape[1]
    bands, rows, _ = wave_ref.shape
    atoms_all = rank_ref.shape[0]
    atoms_dev = d_ref.shape[1]
    kinds = bands * nproj
    height = kinds + 8
    copies = [pltpu.make_async_copy(idx_hbm, idx_ref, sems.at[0])]
    copies += [pltpu.make_async_copy(wave_hbm.at[n], wave_ref.at[n], sems.at[1 + n]) for n in range(bands)]
    copies.append(pltpu.make_async_copy(val_hbm, val_ref, sems.at[1 + bands]))
    copies.append(pltpu.make_async_copy(d_hbm, d_ref, sems.at[2 + bands]))
    copies.append(pltpu.make_async_copy(q_hbm, q_ref, sems.at[3 + bands]))
    for copy in copies:
        copy.start()
    halves = [slice(j, j + LANES) for j in range(0, points, LANES)]
    me = me_ref[0]
    first = (me & (HALF - 1)) * slots
    lane = lax.broadcasted_iota(jnp.int32, (kinds, LANES), 1) - first
    lane_row = lax.broadcasted_iota(jnp.int32, (8, LANES), 1) - first
    out_ref[:height, :] = jnp.zeros((height, LANES), F32)
    pos_ref[...] = jnp.zeros_like(pos_ref)
    col_ref[...] = jnp.full_like(col_ref, -1.0)
    sub_lo = bf(lax.broadcasted_iota(jnp.int32, (LANES, points), 0))
    for copy in copies[2 + bands :]:
        copy.wait()
    matrices = jnp.concatenate([d_ref[...], q_ref[...]], axis=0)
    matrices = jnp.concatenate(
        [matrices, jnp.zeros((matrices.shape[0], LANES - atoms_dev), F32)], axis=1
    )
    out_ref[height:, :] = matrices.T[:atoms_dev]
    for n in range(bands):
        copies[1 + n].wait()
        w = wave_ref[n]
        big = w.astype(BF16)
        grid_ref[rows * n : rows * n + rows, :LANES] = big
        grid_ref[rows * n : rows * n + rows, LANES:] = (w - big.astype(F32)).astype(BF16)
    copies[0].wait()
    copies[1 + bands].wait()
    dense = chunk - aside

    def close(s, accs, sub):
        atom = slot_ref[s]
        live = atom < atoms_all
        pos = rank_ref[jnp.minimum(atom, atoms_all - 1)]
        owner = pos // atoms_dev
        apart = owner ^ me
        block = jnp.where(apart < RING, HALF, HALF + 2) + (apart & 1)
        block = jnp.where(apart < HALF, apart, block)
        column = jnp.where(live, block * atoms_dev + pos - owner * atoms_dev, -1).astype(F32)
        place = jnp.where(live, pos + 1, 0).astype(F32)
        pos_ref[pl.ds(s, 1), :] = jnp.full((1, LANES), place, F32)
        col_ref[pl.ds(s, 1), :] = jnp.full((1, LANES), column, F32)
        out_ref[kinds:height, :] = jnp.where(lane_row == s, place, out_ref[kinds:height, :])
        cols = []
        for n in range(bands):
            total = None
            for acc, h in zip(accs[n], halves, strict=True):
                pick = jnp.take_along_axis(acc, sub[:, h], axis=0, mode="promise_in_bounds")
                prod = pick * val_ref[s, :, h]
                total = prod if total is None else total + prod
            cols.append(jnp.sum(total, axis=1, keepdims=True))
        col = jnp.concatenate(cols, axis=0)
        out_ref[:kinds, :] = jnp.where(lane == s, col, out_ref[:kinds, :])

    def split(s):
        idx = jnp.broadcast_to(idx_ref[pl.ds(s, 1), :], (8, points))
        return idx >> 10, (idx >> 7) & 7, idx & 127

    def body(c, carry):
        @pl.when(slot_ref[c * chunk] < atoms_all)
        def _():
            for j in range(dense):
                idx = idx_ref[pl.ds(c * chunk + j, 1), :]
                hot = jnp.where(sub_lo == bf(idx & 127), jnp.ones((), BF16), jnp.zeros((), BF16))
                hot_ref[:LANES, points * j : points * j + points] = hot
                hot_ref[LANES:, points * j : points * j + points] = hot
            lines = jnp.dot(grid_ref[...], hot_ref[...], preferred_element_type=F32)
            for j in range(dense):
                s = c * chunk + j
                tile, sub, _ = split(s)
                span = slice(points * j, points * j + points)
                accs = []
                for n in range(bands):
                    at = rows * n
                    acc = lines[at : at + 8, span]
                    for k in range(1, rows // 8):
                        acc = jnp.where(tile == k, lines[at + 8 * k : at + 8 * k + 8, span], acc)
                    accs.append([acc[:, h] for h in halves])
                close(s, accs, sub)
            for j in range(dense, chunk):
                s = c * chunk + j
                tile, sub, lo = split(s)
                accs = [[None] * len(halves) for _ in range(bands)]
                for i, h in enumerate(halves):
                    for k in range(rows // 8):
                        hit = tile[:, h] == k
                        for n in range(bands):
                            line = jnp.take_along_axis(
                                wave_ref[n, 8 * k : 8 * k + 8, :], lo[:, h], axis=1, mode="promise_in_bounds"
                            )
                            accs[n][i] = line if k == 0 else jnp.where(hit, line, accs[n][i])
                close(s, accs, sub)

        return carry

    lax.fori_loop(0, slots // chunk, body, 0)


def finish_kernel(me_ref, energy_ref, wave_ref, inner_ref, outer_ref, pot_ref, add_ref, out_hbm, out_ref, sems):
    bands, planes, ny, nz = wave_ref.shape
    even = (me_ref[0] & 1) == 0

    def side(lower, n, p):
        at = (n * 2 + p) * ny
        inner = inner_ref[at : at + ny, :]
        outer = outer_ref[at : at + ny, :]
        return jnp.where(even, outer, inner) if lower else jnp.where(even, inner, outer)

    copies = []
    for n in range(bands):
        padded = [side(True, n, 0), side(True, n, 1)]
        padded += [wave_ref[n, x] for x in range(planes)]
        padded += [side(False, n, 0), side(False, n, 1)]
        for x in range(planes):
            f = padded[x + 2]
            near = padded[x + 1] + padded[x + 3]
            far = padded[x] + padded[x + 4]
            near += pltpu.roll(f, 1, 0) + pltpu.roll(f, ny - 1, 0)
            near += pltpu.roll(f, 1, 1) + pltpu.roll(f, nz - 1, 1)
            far += pltpu.roll(f, 2, 0) + pltpu.roll(f, ny - 2, 0)
            far += pltpu.roll(f, 2, 1) + pltpu.roll(f, nz - 2, 1)
            scale = pot_ref[x] + (3.75 - energy_ref[n])
            added = add_ref[n, ny * x : ny * x + ny, :]
            out_ref[n, x] = added + (scale * f - (2.0 / 3.0) * near + (1.0 / 24.0) * far)
        copy = pltpu.make_async_copy(out_ref.at[n], out_hbm.at[n], sems.at[n])
        copy.start()
        copies.append(copy)
    for copy in copies:
        copy.wait()


def scatter_kernel(
    chunk, atoms_all, energy_ref, slot_ref, own_ref, second_ref, across_ref, beyond_ref,
    pos_ref, col_ref, idx_ref, val_ref, out_ref, a_ref, b_ref, acc_ref, w_ref
):
    slots, points = idx_ref.shape
    nproj = val_ref.shape[1]
    bands, rows, _ = out_ref.shape
    kinds = bands * nproj
    height = kinds + 8
    total = None
    for ref in (own_ref, across_ref, beyond_ref):
        same = jnp.where(pos_ref[...] == ref[kinds : kinds + 1, :], 1.0, 0.0).astype(F32)
        part = lax.dot_general(
            ref[:kinds, :], same, (((1,), (1,)), ((), ())), precision=HIGH, preferred_element_type=F32
        )
        total = part if total is None else total + part
    window = jnp.concatenate(
        [ref[height:, :] for ref in (own_ref, second_ref, across_ref, beyond_ref)], axis=0
    )
    place = lax.broadcasted_iota(jnp.int32, (slots, window.shape[0]), 1).astype(F32)
    mine = jnp.where(col_ref[:, :1] == place, 1.0, 0.0).astype(F32)
    picked = jnp.dot(mine, window, precision=HIGH, preferred_element_type=F32)
    matrices = picked.T
    square = nproj * nproj
    for n in range(bands):
        energy = energy_ref[n]
        mine_n = total[nproj * n : nproj * n + nproj]
        for i in range(nproj):
            at = nproj * i
            mixed = matrices[at : at + nproj] - energy * matrices[square + at : square + at + nproj]
            w_ref[nproj * n + i : nproj * n + i + 1, 0:slots] = jnp.sum(mixed * mine_n, axis=0, keepdims=True)

    lane = lax.broadcasted_iota(jnp.int32, (kinds, slots), 1)
    sub_lo = bf(lax.broadcasted_iota(jnp.int32, (LANES, points), 0))
    sub_hi = bf(lax.broadcasted_iota(jnp.int32, (rows, points), 0))
    zero = jnp.zeros((), BF16)
    one = jnp.ones((), BF16)
    piece = bands * LANES

    def build(s, base):
        idx = idx_ref[pl.ds(s, 1), :]
        lo = bf(idx & 127)
        hi = bf(idx >> 7)
        a_ref[:, base : base + points] = jnp.where(sub_hi == hi, one, zero)
        col = jnp.sum(jnp.where(lane == s, w_ref[:, 0:slots], 0.0), axis=1, keepdims=True)
        v = val_ref[s]
        hit = sub_lo == lo
        for n in range(bands):
            back = jnp.sum(col[nproj * n : nproj * n + nproj] * v, axis=0, keepdims=True)
            big = back.astype(BF16)
            small = (back - big.astype(F32)).astype(BF16)
            at = LANES * n
            b_ref[at : at + LANES, base : base + points] = jnp.where(hit, big, zero)
            b_ref[piece + at : piece + at + LANES, base : base + points] = jnp.where(hit, small, zero)

    acc_ref[...] = jnp.zeros_like(acc_ref)

    def body(c, carry):
        @pl.when(slot_ref[c * chunk] < atoms_all)
        def _():
            for j in range(chunk):
                build(c * chunk + j, points * j)
            acc_ref[...] += lax.dot_general(
                b_ref[...], a_ref[...], (((1,), (1,)), ((), ())), preferred_element_type=F32
            )

        return carry

    lax.fori_loop(0, slots // chunk, body, 0)
    for n in range(bands):
        at = LANES * n
        out_ref[n] = (acc_ref[at : at + LANES] + acc_ref[piece + at : piece + at + LANES]).T


def swapped(value, partner):
    count = lax.axis_size("dom")
    return lax.ppermute(value, "dom", [(s, partner(s) % count) for s in range(count)])


def inner_of(d):
    return d ^ 1


def outer_of(d):
    return d + 1 if d % 2 else d - 1


def second_of(d):
    return d ^ 2


def across_of(d):
    base, y = d - d % RING, d % RING
    return base + (6, 7, 4, 5, 2, 3, 0, 1)[y]


def beyond_of(d):
    base, y = d - d % RING, d % RING
    if y < HALF:
        return base - RING + (6, 7, 4, 5)[y]
    return base + RING + (2, 3, 0, 1)[y - HALF]


def per_device(
    wave, potential, energies, proj_index, proj_values, slot_atom, atom_rank, d_matrix, q_matrix
):
    bands, planes, ny, nz = wave.shape
    slots, points = proj_index.shape
    nproj = proj_values.shape[1]
    atoms_dev = d_matrix.shape[0]
    atoms_all = atom_rank.shape[0]
    kinds = bands * nproj
    rows = planes * ny
    me = lax.axis_index("dom").astype(jnp.int32).reshape(1)
    flat = wave.reshape(bands, rows, nz)
    edge = bands * 2 * ny
    height = kinds + 8
    square = nproj * nproj

    def turned(m):
        return jnp.transpose(m, (1, 2, 0)).reshape(square, atoms_dev)

    chunk, aside = 16, 4
    mine, pos, col = pl.pallas_call(
        functools.partial(gather_kernel, chunk, aside),
        out_shape=(
            jax.ShapeDtypeStruct((height + atoms_dev, LANES), F32),
            jax.ShapeDtypeStruct((slots, LANES), F32),
            jax.ShapeDtypeStruct((slots, LANES), F32),
        ),
        in_specs=[SMEM, SMEM, SMEM, HBM, HBM, HBM, HBM, HBM],
        out_specs=(VMEM, VMEM, VMEM),
        scratch_shapes=[
            pltpu.VMEM(proj_index.shape, jnp.int32),
            pltpu.VMEM(proj_values.shape, F32),
            pltpu.VMEM(flat.shape, F32),
            pltpu.VMEM((square, atoms_dev), F32),
            pltpu.VMEM((square, atoms_dev), F32),
            pltpu.VMEM((bands * rows, 2 * LANES), BF16),
            pltpu.VMEM((2 * LANES, points * (chunk - aside)), BF16),
            pltpu.SemaphoreType.DMA((4 + bands,)),
        ],
        compiler_params=pltpu.CompilerParams(vmem_limit_bytes=40 * MIB),
        cost_estimate=pl.CostEstimate(flops=10**10, bytes_accessed=10**7, transcendentals=0),
        name="gather",
    )(me, kept(slot_atom), kept(atom_rank), kept(proj_index), kept(proj_values), kept(flat), kept(turned(d_matrix)), kept(turned(q_matrix)))

    first = swapped(mine, inner_of)
    pair = mine[:height] + first[:height]
    known = [mine[height:], first[height:]]
    second = swapped(jnp.concatenate([pair] + known, axis=0), second_of)
    half = jnp.concatenate([pair + second[:height]] + known, axis=0)

    inner, outer = pl.pallas_call(
        pack_kernel,
        out_shape=(jax.ShapeDtypeStruct((edge, nz), F32),) * 2,
        in_specs=[SMEM, HBM, pl.BlockSpec(memory_space=pl.ANY)],
        out_specs=(VMEM, VMEM),
        scratch_shapes=[pltpu.SemaphoreType.DMA((2, bands))],
        compiler_params=pltpu.CompilerParams(vmem_limit_bytes=4 * MIB),
        cost_estimate=pl.CostEstimate(flops=10**6, bytes_accessed=10**6, transcendentals=0),
        name="pack",
    )(me, kept(flat), col)
    beyond = swapped(half, beyond_of)
    across = swapped(half, across_of)
    outer_got = swapped(outer, outer_of)
    inner_got = swapped(inner, inner_of)

    chunk = 16
    added = pl.pallas_call(
        functools.partial(scatter_kernel, chunk, atoms_all),
        out_shape=jax.ShapeDtypeStruct((bands, rows, nz), F32),
        in_specs=[SMEM, SMEM] + [VMEM] * 8,
        out_specs=VMEM,
        scratch_shapes=[
            pltpu.VMEM((rows, points * chunk), BF16),
            pltpu.VMEM((2 * bands * LANES, points * chunk), BF16),
            pltpu.VMEM((2 * bands * LANES, rows), F32),
            pltpu.VMEM((kinds, LANES), F32),
        ],
        compiler_params=pltpu.CompilerParams(vmem_limit_bytes=40 * MIB),
        cost_estimate=pl.CostEstimate(flops=10**10, bytes_accessed=10**7, transcendentals=0),
        name="scatter",
    )(kept(energies), kept(slot_atom), half, second, across, beyond, pos, col, proj_index, proj_values)

    return pl.pallas_call(
        finish_kernel,
        out_shape=jax.ShapeDtypeStruct(wave.shape, F32),
        in_specs=[SMEM, SMEM, VMEM, VMEM, VMEM, VMEM, VMEM],
        out_specs=HBM,
        scratch_shapes=[pltpu.VMEM(wave.shape, F32), pltpu.SemaphoreType.DMA((bands,))],
        compiler_params=pltpu.CompilerParams(vmem_limit_bytes=8 * MIB),
        name="finish",
    )(me, energies, wave, inner_got, outer_got, potential, added)


def solution(mesh):
    placed = (
        P("band", "dom", None, None),
        P("dom", None, None),
        P("band"),
        P("dom", None),
        P("dom", None, None),
        P("dom"),
        P(),
        P("dom", None, None),
        P("dom", None, None),
    )
    return jax.shard_map(
        per_device,
        mesh=mesh,
        in_specs=placed,
        out_specs=P("band", "dom", None, None),
        check_vma=False,
    )
```

```python
import functools

import jax
import jax.numpy as jnp
from jax import lax
from jax.experimental import pallas as pl
from jax.experimental.pallas import tpu as pltpu
from jax.sharding import PartitionSpec as P


HIGH = lax.Precision.HIGHEST
F32 = jnp.float32
BF16 = jnp.bfloat16
VMEM = pl.BlockSpec(memory_space=pltpu.VMEM)
HBM = pl.BlockSpec(memory_space=pltpu.HBM)
LANES = 128
HALF = 4
RING = 8
MIB = 1 << 20


def kept(x):
    return pltpu.with_memory_space_constraint(x, pltpu.HBM)


def bf(x):
    return x.astype(F32).astype(BF16)


def pack_kernel(wave_hbm, pot_hbm, col_ref, inner_ref, outer_ref, base_ref, wave_ref, pot_ref, sems, edge_sems):
    bands, planes, ny, nz = wave_ref.shape
    half = planes // 2
    whole = [pltpu.make_async_copy(pot_hbm, pot_ref, sems.at[bands])]
    whole += [pltpu.make_async_copy(wave_hbm.at[n], wave_ref.at[n], sems.at[n]) for n in range(bands)]
    even = (lax.axis_index("dom") & 1) == 0
    edges = []
    for index, (ref, upper) in enumerate(((inner_ref, even), (outer_ref, jnp.logical_not(even)))):
        start = jnp.where(upper, half, 0)
        for n in range(bands):
            for p in range(half):
                edges.append(
                    pltpu.make_async_copy(
                        wave_hbm.at[n, start + p],
                        ref.at[pl.ds((n * half + p) * ny, ny), :],
                        edge_sems.at[index, n, p],
                    )
                )
    for copy in edges + whole:
        copy.start()
    whole[0].wait()
    slots = col_ref.shape[0] - 8
    for n in range(bands):
        whole[1 + n].wait()
        energy = col_ref[slots + n : slots + n + 1, :]
        for x in range(planes):
            f = wave_ref[n, x]
            near = pltpu.roll(f, 1, 0) + pltpu.roll(f, ny - 1, 0)
            near += pltpu.roll(f, 1, 1) + pltpu.roll(f, nz - 1, 1)
            far = pltpu.roll(f, 2, 0) + pltpu.roll(f, ny - 2, 0)
            far += pltpu.roll(f, 2, 1) + pltpu.roll(f, nz - 2, 1)
            for step in (-1, 1):
                if 0 <= x + step < planes:
                    near += wave_ref[n, x + step]
                if 0 <= x + 2 * step < planes:
                    far += wave_ref[n, x + 2 * step]
            base_ref[n, x] = (pot_ref[x] + (3.75 - energy)) * f - (2.0 / 3.0) * near + (1.0 / 24.0) * far
    for copy in edges:
        copy.wait()


def gather_kernel(
    chunk, aside, slot_hbm, rank_hbm, energy_hbm, idx_hbm, val_hbm, wave_hbm, d_hbm, q_hbm,
    out_ref, pos_ref, col_ref,
    slot_ref, rank_ref, energy_ref, idx_ref, val_ref, wave_ref, d_ref, q_ref, grid_ref, hot_ref, sems
):
    slots, points = idx_ref.shape
    nproj = val_ref.shape[1]
    bands, rows, _ = wave_ref.shape
    atoms_all = rank_ref.shape[0]
    atoms_dev = d_ref.shape[1]
    kinds = bands * nproj
    height = kinds + 8
    copies = [pltpu.make_async_copy(idx_hbm, idx_ref, sems.at[0])]
    copies += [pltpu.make_async_copy(wave_hbm.at[n], wave_ref.at[n], sems.at[1 + n]) for n in range(bands)]
    copies.append(pltpu.make_async_copy(val_hbm, val_ref, sems.at[1 + bands]))
    copies.append(pltpu.make_async_copy(d_hbm, d_ref, sems.at[2 + bands]))
    copies.append(pltpu.make_async_copy(q_hbm, q_ref, sems.at[3 + bands]))
    scalars = [
        pltpu.make_async_copy(source, ref, sems.at[4 + bands + k])
        for k, (source, ref) in enumerate(
            ((slot_hbm, slot_ref), (energy_hbm, energy_ref), (rank_hbm, rank_ref))
        )
    ]
    for copy in copies + scalars:
        copy.start()
    halves = [slice(j, j + LANES) for j in range(0, points, LANES)]
    me = lax.axis_index("dom")
    first = (me & (HALF - 1)) * slots
    lane = lax.broadcasted_iota(jnp.int32, (kinds, LANES), 1) - first
    lane_row = lax.broadcasted_iota(jnp.int32, (8, LANES), 1) - first
    out_ref[:height, :] = jnp.zeros((height, LANES), F32)
    pos_ref[...] = jnp.zeros_like(pos_ref)
    col_ref[...] = jnp.full_like(col_ref, -1.0)
    sub_lo = bf(lax.broadcasted_iota(jnp.int32, (LANES, points), 0))
    for copy in copies[2 + bands :]:
        copy.wait()
    matrices = jnp.concatenate([d_ref[...], q_ref[...]], axis=0)
    matrices = jnp.concatenate(
        [matrices, jnp.zeros((matrices.shape[0], LANES - atoms_dev), F32)], axis=1
    )
    out_ref[height:, :] = matrices.T[:atoms_dev]
    for n in range(bands):
        copies[1 + n].wait()
        w = wave_ref[n]
        big = w.astype(BF16)
        grid_ref[rows * n : rows * n + rows, :LANES] = big
        grid_ref[rows * n : rows * n + rows, LANES:] = (w - big.astype(F32)).astype(BF16)
    copies[0].wait()
    copies[1 + bands].wait()
    for copy in scalars:
        copy.wait()
    for n in range(bands):
        col_ref[slots + n : slots + n + 1, :] = jnp.full((1, LANES), energy_ref[n], F32)
    dense = chunk - aside

    def close(s, accs, sub):
        atom = slot_ref[s]
        live = atom < atoms_all
        pos = rank_ref[jnp.minimum(atom, atoms_all - 1)]
        owner = pos // atoms_dev
        apart = owner ^ me
        block = jnp.where(apart < RING, HALF, HALF + 2) + (apart & 1)
        block = jnp.where(apart < HALF, apart, block)
        column = jnp.where(live, block * atoms_dev + pos - owner * atoms_dev, -1).astype(F32)
        place = jnp.where(live, pos + 1, 0).astype(F32)
        pos_ref[pl.ds(s, 1), :] = jnp.full((1, LANES), place, F32)
        col_ref[pl.ds(s, 1), :] = jnp.full((1, LANES), column, F32)
        out_ref[kinds:height, :] = jnp.where(lane_row == s, place, out_ref[kinds:height, :])
        cols = []
        for n in range(bands):
            total = None
            for acc, h in zip(accs[n], halves, strict=True):
                pick = jnp.take_along_axis(acc, sub[:, h], axis=0, mode="promise_in_bounds")
                prod = pick * val_ref[s, :, h]
                total = prod if total is None else total + prod
            cols.append(jnp.sum(total, axis=1, keepdims=True))
        col = jnp.concatenate(cols, axis=0)
        out_ref[:kinds, :] = jnp.where(lane == s, col, out_ref[:kinds, :])

    def split(s):
        idx = jnp.broadcast_to(idx_ref[pl.ds(s, 1), :], (8, points))
        return idx >> 10, (idx >> 7) & 7, idx & 127

    def body(c, carry):
        @pl.when(slot_ref[c * chunk] < atoms_all)
        def _():
            for j in range(dense):
                idx = idx_ref[pl.ds(c * chunk + j, 1), :]
                hot = jnp.where(sub_lo == bf(idx & 127), jnp.ones((), BF16), jnp.zeros((), BF16))
                hot_ref[:LANES, points * j : points * j + points] = hot
                hot_ref[LANES:, points * j : points * j + points] = hot
            lines = jnp.dot(grid_ref[...], hot_ref[...], preferred_element_type=F32)
            for j in range(dense):
                s = c * chunk + j
                tile, sub, _ = split(s)
                span = slice(points * j, points * j + points)
                accs = []
                for n in range(bands):
                    at = rows * n
                    acc = lines[at : at + 8, span]
                    for k in range(1, rows // 8):
                        acc = jnp.where(tile == k, lines[at + 8 * k : at + 8 * k + 8, span], acc)
                    accs.append([acc[:, h] for h in halves])
                close(s, accs, sub)
            for j in range(dense, chunk):
                s = c * chunk + j
                tile, sub, lo = split(s)
                accs = [[None] * len(halves) for _ in range(bands)]
                for i, h in enumerate(halves):
                    for k in range(rows // 8):
                        hit = tile[:, h] == k
                        for n in range(bands):
                            line = jnp.take_along_axis(
                                wave_ref[n, 8 * k : 8 * k + 8, :], lo[:, h], axis=1, mode="promise_in_bounds"
                            )
                            accs[n][i] = line if k == 0 else jnp.where(hit, line, accs[n][i])
                close(s, accs, sub)

        return carry

    lax.fori_loop(0, slots // chunk, body, 0)


def finish_kernel(inner_ref, outer_ref, base_ref, add_ref, out_hbm, out_ref, sems):
    bands, planes, ny, _ = base_ref.shape
    half = planes // 2
    even = (lax.axis_index("dom") & 1) == 0

    def side(lower, n, p):
        at = (n * half + p) * ny
        inner = inner_ref[at : at + ny, :]
        outer = outer_ref[at : at + ny, :]
        return jnp.where(even, outer, inner) if lower else jnp.where(even, inner, outer)

    copies = []
    for n in range(bands):
        halo = {-2: side(True, n, 0), -1: side(True, n, 1), planes: side(False, n, 0), planes + 1: side(False, n, 1)}
        for x in range(planes):
            value = add_ref[n, ny * x : ny * x + ny, :] + base_ref[n, x]
            for step in (-1, 1):
                if x + step in halo:
                    value -= (2.0 / 3.0) * halo[x + step]
                if x + 2 * step in halo:
                    value += (1.0 / 24.0) * halo[x + 2 * step]
            out_ref[n, x] = value
        copy = pltpu.make_async_copy(out_ref.at[n], out_hbm.at[n], sems.at[n])
        copy.start()
        copies.append(copy)
    for copy in copies:
        copy.wait()


def scatter_kernel(
    chunk, own_ref, second_ref, across_ref, beyond_ref,
    pos_ref, col_ref, idx_ref, val_ref, out_ref, a_ref, b_ref, acc_ref, w_ref
):
    slots, points = idx_ref.shape
    nproj = val_ref.shape[1]
    bands, rows, _ = out_ref.shape
    kinds = bands * nproj
    height = kinds + 8
    steps = jnp.int32(0)
    for c in range(slots // chunk):
        live = jnp.max(pos_ref[c * chunk : c * chunk + 1, :]) > 0
        steps = steps + live.astype(jnp.int32)
    total = None
    for ref in (own_ref, across_ref, beyond_ref):
        same = jnp.where(pos_ref[...] == ref[kinds : kinds + 1, :], 1.0, 0.0).astype(F32)
        part = lax.dot_general(
            ref[:kinds, :], same, (((1,), (1,)), ((), ())), precision=HIGH, preferred_element_type=F32
        )
        total = part if total is None else total + part
    window = jnp.concatenate(
        [ref[height:, :] for ref in (own_ref, second_ref, across_ref, beyond_ref)], axis=0
    )
    place = lax.broadcasted_iota(jnp.int32, (slots, window.shape[0]), 1).astype(F32)
    mine = jnp.where(col_ref[:slots, :1] == place, 1.0, 0.0).astype(F32)
    picked = jnp.dot(mine, window, precision=HIGH, preferred_element_type=F32)
    matrices = picked.T
    square = nproj * nproj
    for n in range(bands):
        energy = col_ref[slots + n : slots + n + 1, :slots]
        mine_n = total[nproj * n : nproj * n + nproj]
        for i in range(nproj):
            at = nproj * i
            mixed = matrices[at : at + nproj] - energy * matrices[square + at : square + at + nproj]
            w_ref[nproj * n + i : nproj * n + i + 1, 0:slots] = jnp.sum(mixed * mine_n, axis=0, keepdims=True)

    lane = lax.broadcasted_iota(jnp.int32, (kinds, slots), 1)
    sub_lo = bf(lax.broadcasted_iota(jnp.int32, (LANES, points), 0))
    sub_hi = bf(lax.broadcasted_iota(jnp.int32, (rows, points), 0))
    zero = jnp.zeros((), BF16)
    one = jnp.ones((), BF16)
    piece = bands * LANES

    def build(s, base):
        idx = idx_ref[pl.ds(s, 1), :]
        lo = bf(idx & 127)
        hi = bf(idx >> 7)
        a_ref[:, base : base + points] = jnp.where(sub_hi == hi, one, zero)
        col = jnp.sum(jnp.where(lane == s, w_ref[:, 0:slots], 0.0), axis=1, keepdims=True)
        v = val_ref[s]
        hit = sub_lo == lo
        for n in range(bands):
            back = jnp.sum(col[nproj * n : nproj * n + nproj] * v, axis=0, keepdims=True)
            big = back.astype(BF16)
            small = (back - big.astype(F32)).astype(BF16)
            at = LANES * n
            b_ref[at : at + LANES, base : base + points] = jnp.where(hit, big, zero)
            b_ref[piece + at : piece + at + LANES, base : base + points] = jnp.where(hit, small, zero)

    acc_ref[...] = jnp.zeros_like(acc_ref)

    def body(c, carry):
        for j in range(chunk):
            build(c * chunk + j, points * j)
        acc_ref[...] += lax.dot_general(
            b_ref[...], a_ref[...], (((1,), (1,)), ((), ())), preferred_element_type=F32
        )
        return carry

    lax.fori_loop(0, steps, body, 0)
    for n in range(bands):
        at = LANES * n
        out_ref[n] = (acc_ref[at : at + LANES] + acc_ref[piece + at : piece + at + LANES]).T


def swapped(value, partner):
    count = lax.axis_size("dom")
    return lax.ppermute(value, "dom", [(s, partner(s) % count) for s in range(count)])


def inner_of(d):
    return d ^ 1


def outer_of(d):
    return d + 1 if d % 2 else d - 1


def second_of(d):
    return d ^ 2


def across_of(d):
    base, y = d - d % RING, d % RING
    return base + (6, 7, 4, 5, 2, 3, 0, 1)[y]


def beyond_of(d):
    base, y = d - d % RING, d % RING
    if y < HALF:
        return base - RING + (6, 7, 4, 5)[y]
    return base + RING + (2, 3, 0, 1)[y - HALF]


def per_device(
    wave, potential, energies, proj_index, proj_values, slot_atom, atom_rank, d_matrix, q_matrix
):
    bands, planes, ny, nz = wave.shape
    slots, points = proj_index.shape
    nproj = proj_values.shape[1]
    atoms_dev = d_matrix.shape[0]
    kinds = bands * nproj
    rows = planes * ny
    flat = wave.reshape(bands, rows, nz)
    edge = bands * 2 * ny
    height = kinds + 8
    square = nproj * nproj

    def turned(m):
        return jnp.transpose(m, (1, 2, 0)).reshape(square, atoms_dev)

    chunk, aside = 16, 4
    mine, pos, col = pl.pallas_call(
        functools.partial(gather_kernel, chunk, aside),
        out_shape=(
            jax.ShapeDtypeStruct((height + atoms_dev, LANES), F32),
            jax.ShapeDtypeStruct((slots, LANES), F32),
            jax.ShapeDtypeStruct((slots + 8, LANES), F32),
        ),
        in_specs=[HBM] * 8,
        out_specs=(VMEM, VMEM, VMEM),
        scratch_shapes=[
            pltpu.SMEM(slot_atom.shape, jnp.int32),
            pltpu.SMEM(atom_rank.shape, jnp.int32),
            pltpu.SMEM(energies.shape, F32),
            pltpu.VMEM(proj_index.shape, jnp.int32),
            pltpu.VMEM(proj_values.shape, F32),
            pltpu.VMEM(flat.shape, F32),
            pltpu.VMEM((square, atoms_dev), F32),
            pltpu.VMEM((square, atoms_dev), F32),
            pltpu.VMEM((bands * rows, 2 * LANES), BF16),
            pltpu.VMEM((2 * LANES, points * (chunk - aside)), BF16),
            pltpu.SemaphoreType.DMA((7 + bands,)),
        ],
        compiler_params=pltpu.CompilerParams(vmem_limit_bytes=40 * MIB),
        cost_estimate=pl.CostEstimate(flops=10**10, bytes_accessed=10**7, transcendentals=0),
        name="gather",
    )(
        *[
            kept(x)
            for x in (
                slot_atom, atom_rank, energies, proj_index, proj_values, flat, turned(d_matrix), turned(q_matrix)
            )
        ]
    )

    first = swapped(mine, inner_of)
    pair = mine[:height] + first[:height]
    known = [mine[height:], first[height:]]
    second = swapped(jnp.concatenate([pair] + known, axis=0), second_of)
    half = jnp.concatenate([pair + second[:height]] + known, axis=0)

    inner, outer, base = pl.pallas_call(
        pack_kernel,
        out_shape=(jax.ShapeDtypeStruct((edge, nz), F32),) * 2 + (jax.ShapeDtypeStruct(wave.shape, F32),),
        in_specs=[HBM, HBM, VMEM],
        out_specs=(VMEM, VMEM, VMEM),
        scratch_shapes=[
            pltpu.VMEM(wave.shape, F32),
            pltpu.VMEM(potential.shape, F32),
            pltpu.SemaphoreType.DMA((bands + 1,)),
            pltpu.SemaphoreType.DMA((2, bands, planes // 2)),
        ],
        compiler_params=pltpu.CompilerParams(vmem_limit_bytes=8 * MIB),
        cost_estimate=pl.CostEstimate(flops=10**6, bytes_accessed=10**6, transcendentals=0),
        name="pack",
    )(kept(wave), kept(potential), col)
    beyond = swapped(half, beyond_of)
    across = swapped(half, across_of)
    outer_got = swapped(outer, outer_of)
    inner_got = swapped(inner, inner_of)

    chunk = 16
    added = pl.pallas_call(
        functools.partial(scatter_kernel, chunk),
        out_shape=jax.ShapeDtypeStruct((bands, rows, nz), F32),
        in_specs=[VMEM] * 8,
        out_specs=VMEM,
        scratch_shapes=[
            pltpu.VMEM((rows, points * chunk), BF16),
            pltpu.VMEM((2 * bands * LANES, points * chunk), BF16),
            pltpu.VMEM((2 * bands * LANES, rows), F32),
            pltpu.VMEM((kinds, LANES), F32),
        ],
        compiler_params=pltpu.CompilerParams(vmem_limit_bytes=40 * MIB),
        cost_estimate=pl.CostEstimate(flops=10**10, bytes_accessed=10**7, transcendentals=0),
        name="scatter",
    )(half, second, across, beyond, pos, col, proj_index, proj_values)

    return pl.pallas_call(
        finish_kernel,
        out_shape=jax.ShapeDtypeStruct(wave.shape, F32),
        in_specs=[VMEM] * 4,
        out_specs=HBM,
        scratch_shapes=[pltpu.VMEM(wave.shape, F32), pltpu.SemaphoreType.DMA((bands,))],
        compiler_params=pltpu.CompilerParams(vmem_limit_bytes=8 * MIB),
        name="finish",
    )(inner_got, outer_got, base, added)


def solution(mesh):
    placed = (
        P("band", "dom", None, None),
        P("dom", None, None),
        P("band"),
        P("dom", None),
        P("dom", None, None),
        P("dom"),
        P(),
        P("dom", None, None),
        P("dom", None, None),
    )
    return jax.shard_map(
        per_device,
        mesh=mesh,
        in_specs=placed,
        out_specs=P("band", "dom", None, None),
        check_vma=False,
    )
```

```python
import functools

import jax
import jax.numpy as jnp
from jax import lax
from jax.experimental import pallas as pl
from jax.experimental.pallas import tpu as pltpu
from jax.sharding import PartitionSpec as P


HIGH = lax.Precision.HIGHEST
F32 = jnp.float32
BF16 = jnp.bfloat16
VMEM = pl.BlockSpec(memory_space=pltpu.VMEM)
HBM = pl.BlockSpec(memory_space=pltpu.HBM)
LANES = 128
HALF = 4
RING = 8
MIB = 1 << 20


def kept(x):
    return pltpu.with_memory_space_constraint(x, pltpu.HBM)


def bf(x):
    return x.astype(F32).astype(BF16)


def pack_kernel(wave_hbm, pot_hbm, col_ref, inner_ref, outer_ref, base_ref, wave_ref, pot_ref, sems, edge_sems):
    bands, planes, ny, nz = wave_ref.shape
    half = planes // 2
    whole = [pltpu.make_async_copy(pot_hbm, pot_ref, sems.at[bands])]
    whole += [pltpu.make_async_copy(wave_hbm.at[n], wave_ref.at[n], sems.at[n]) for n in range(bands)]
    even = (lax.axis_index("dom") & 1) == 0
    edges = []
    for index, (ref, upper) in enumerate(((inner_ref, even), (outer_ref, jnp.logical_not(even)))):
        start = jnp.where(upper, half, 0)
        for n in range(bands):
            for p in range(half):
                edges.append(
                    pltpu.make_async_copy(
                        wave_hbm.at[n, start + p],
                        ref.at[pl.ds((n * half + p) * ny, ny), :],
                        edge_sems.at[index, n, p],
                    )
                )
    for copy in edges + whole:
        copy.start()
    whole[0].wait()
    slots = col_ref.shape[0] - 8
    for n in range(bands):
        whole[1 + n].wait()
        energy = col_ref[slots + n : slots + n + 1, :]
        for x in range(planes):
            f = wave_ref[n, x]
            near = pltpu.roll(f, 1, 0) + pltpu.roll(f, ny - 1, 0)
            near += pltpu.roll(f, 1, 1) + pltpu.roll(f, nz - 1, 1)
            far = pltpu.roll(f, 2, 0) + pltpu.roll(f, ny - 2, 0)
            far += pltpu.roll(f, 2, 1) + pltpu.roll(f, nz - 2, 1)
            for step in (-1, 1):
                if 0 <= x + step < planes:
                    near += wave_ref[n, x + step]
                if 0 <= x + 2 * step < planes:
                    far += wave_ref[n, x + 2 * step]
            base_ref[n, x] = (pot_ref[x] + (3.75 - energy)) * f - (2.0 / 3.0) * near + (1.0 / 24.0) * far
    for copy in edges:
        copy.wait()


def gather_kernel(
    chunk, aside, slot_hbm, rank_hbm, energy_hbm, idx_hbm, val_hbm, wave_hbm, d_hbm, q_hbm,
    many_ref, pos_ref, col_ref,
    out_ref, slot_ref, rank_ref, energy_ref, idx_ref, val_ref, wave_ref, d_ref, q_ref, grid_ref, hot_ref, sems
):
    slots, points = idx_ref.shape
    nproj = val_ref.shape[1]
    bands, rows, _ = wave_ref.shape
    atoms_all = rank_ref.shape[0]
    atoms_dev = d_ref.shape[1]
    kinds = bands * nproj
    height = kinds + 8
    copies = [pltpu.make_async_copy(idx_hbm, idx_ref, sems.at[0])]
    copies += [pltpu.make_async_copy(wave_hbm.at[n], wave_ref.at[n], sems.at[1 + n]) for n in range(bands)]
    copies.append(pltpu.make_async_copy(val_hbm, val_ref, sems.at[1 + bands]))
    copies.append(pltpu.make_async_copy(d_hbm, d_ref, sems.at[2 + bands]))
    copies.append(pltpu.make_async_copy(q_hbm, q_ref, sems.at[3 + bands]))
    scalars = [
        pltpu.make_async_copy(source, ref, sems.at[4 + bands + k])
        for k, (source, ref) in enumerate(
            ((slot_hbm, slot_ref), (energy_hbm, energy_ref), (rank_hbm, rank_ref))
        )
    ]
    for copy in copies + scalars:
        copy.start()
    halves = [slice(j, j + LANES) for j in range(0, points, LANES)]
    me = lax.axis_index("dom")
    first = (me & (HALF - 1)) * slots
    lane = lax.broadcasted_iota(jnp.int32, (kinds, LANES), 1) - first
    lane_row = lax.broadcasted_iota(jnp.int32, (8, LANES), 1) - first
    out_ref[:height, :] = jnp.zeros((height, LANES), F32)
    pos_ref[...] = jnp.zeros_like(pos_ref)
    col_ref[...] = jnp.full_like(col_ref, -1.0)
    sub_lo = bf(lax.broadcasted_iota(jnp.int32, (LANES, points), 0))
    for copy in copies[2 + bands :]:
        copy.wait()
    matrices = jnp.concatenate([d_ref[...], q_ref[...]], axis=0)
    matrices = jnp.concatenate(
        [matrices, jnp.zeros((matrices.shape[0], LANES - atoms_dev), F32)], axis=1
    )
    out_ref[height:, :] = matrices.T[:atoms_dev]
    for n in range(bands):
        copies[1 + n].wait()
        w = wave_ref[n]
        big = w.astype(BF16)
        grid_ref[rows * n : rows * n + rows, :LANES] = big
        grid_ref[rows * n : rows * n + rows, LANES:] = (w - big.astype(F32)).astype(BF16)
    copies[0].wait()
    copies[1 + bands].wait()
    for copy in scalars:
        copy.wait()
    for n in range(bands):
        col_ref[slots + n : slots + n + 1, :] = jnp.full((1, LANES), energy_ref[n], F32)
    dense = chunk - aside

    def close(s, accs, sub):
        atom = slot_ref[s]
        live = atom < atoms_all
        pos = rank_ref[jnp.minimum(atom, atoms_all - 1)]
        owner = pos // atoms_dev
        apart = owner ^ me
        block = jnp.where(apart < RING, HALF, HALF + 2) + (owner & 1)
        block = jnp.where(apart < HALF, owner & (HALF - 1), block)
        column = jnp.where(live, block * atoms_dev + pos - owner * atoms_dev, -1).astype(F32)
        place = jnp.where(live, pos + 1, 0).astype(F32)
        pos_ref[pl.ds(s, 1), :] = jnp.full((1, LANES), place, F32)
        col_ref[pl.ds(s, 1), :] = jnp.full((1, LANES), column, F32)
        out_ref[kinds:height, :] = jnp.where(lane_row == s, place, out_ref[kinds:height, :])
        cols = []
        for n in range(bands):
            total = None
            for acc, h in zip(accs[n], halves, strict=True):
                pick = jnp.take_along_axis(acc, sub[:, h], axis=0, mode="promise_in_bounds")
                prod = pick * val_ref[s, :, h]
                total = prod if total is None else total + prod
            cols.append(jnp.sum(total, axis=1, keepdims=True))
        col = jnp.concatenate(cols, axis=0)
        out_ref[:kinds, :] = jnp.where(lane == s, col, out_ref[:kinds, :])

    def split(s):
        idx = jnp.broadcast_to(idx_ref[pl.ds(s, 1), :], (8, points))
        return idx >> 10, (idx >> 7) & 7, idx & 127

    def body(c, carry):
        @pl.when(slot_ref[c * chunk] < atoms_all)
        def _():
            for j in range(dense):
                idx = idx_ref[pl.ds(c * chunk + j, 1), :]
                hot = jnp.where(sub_lo == bf(idx & 127), jnp.ones((), BF16), jnp.zeros((), BF16))
                hot_ref[:LANES, points * j : points * j + points] = hot
                hot_ref[LANES:, points * j : points * j + points] = hot
            lines = jnp.dot(grid_ref[...], hot_ref[...], preferred_element_type=F32)
            for j in range(dense):
                s = c * chunk + j
                tile, sub, _ = split(s)
                span = slice(points * j, points * j + points)
                accs = []
                for n in range(bands):
                    at = rows * n
                    acc = lines[at : at + 8, span]
                    for k in range(1, rows // 8):
                        acc = jnp.where(tile == k, lines[at + 8 * k : at + 8 * k + 8, span], acc)
                    accs.append([acc[:, h] for h in halves])
                close(s, accs, sub)
            for j in range(dense, chunk):
                s = c * chunk + j
                tile, sub, lo = split(s)
                accs = [[None] * len(halves) for _ in range(bands)]
                for i, h in enumerate(halves):
                    for k in range(rows // 8):
                        hit = tile[:, h] == k
                        for n in range(bands):
                            line = jnp.take_along_axis(
                                wave_ref[n, 8 * k : 8 * k + 8, :], lo[:, h], axis=1, mode="promise_in_bounds"
                            )
                            accs[n][i] = line if k == 0 else jnp.where(hit, line, accs[n][i])
                close(s, accs, sub)

        return carry

    lax.fori_loop(0, slots // chunk, body, 0)
    for k in range(many_ref.shape[0]):
        many_ref[k] = out_ref[...]


def finish_kernel(inner_ref, outer_ref, base_ref, add_ref, out_hbm, out_ref, sems):
    bands, planes, ny, _ = base_ref.shape
    half = planes // 2
    even = (lax.axis_index("dom") & 1) == 0

    def side(lower, n, p):
        at = (n * half + p) * ny
        inner = inner_ref[at : at + ny, :]
        outer = outer_ref[at : at + ny, :]
        return jnp.where(even, outer, inner) if lower else jnp.where(even, inner, outer)

    copies = []
    for n in range(bands):
        halo = {-2: side(True, n, 0), -1: side(True, n, 1), planes: side(False, n, 0), planes + 1: side(False, n, 1)}
        for x in range(planes):
            value = add_ref[n, ny * x : ny * x + ny, :] + base_ref[n, x]
            for step in (-1, 1):
                if x + step in halo:
                    value -= (2.0 / 3.0) * halo[x + step]
                if x + 2 * step in halo:
                    value += (1.0 / 24.0) * halo[x + 2 * step]
            out_ref[n, x] = value
        copy = pltpu.make_async_copy(out_ref.at[n], out_hbm.at[n], sems.at[n])
        copy.start()
        copies.append(copy)
    for copy in copies:
        copy.wait()


def scatter_kernel(
    chunk, own_ref, quads_ref, across_ref, beyond_ref,
    pos_ref, col_ref, idx_ref, val_ref, out_ref, a_ref, b_ref, acc_ref, w_ref
):
    slots, points = idx_ref.shape
    nproj = val_ref.shape[1]
    bands, rows, _ = out_ref.shape
    kinds = bands * nproj
    height = kinds + 8
    steps = jnp.int32(0)
    for c in range(slots // chunk):
        live = jnp.max(pos_ref[c * chunk : c * chunk + 1, :]) > 0
        steps = steps + live.astype(jnp.int32)
    total = None
    for ref in (own_ref, across_ref, beyond_ref):
        same = jnp.where(pos_ref[...] == ref[kinds : kinds + 1, :], 1.0, 0.0).astype(F32)
        part = lax.dot_general(
            ref[:kinds, :], same, (((1,), (1,)), ((), ())), precision=HIGH, preferred_element_type=F32
        )
        total = part if total is None else total + part
    window = jnp.concatenate(
        [quads_ref[...], across_ref[height:, :], beyond_ref[height:, :]], axis=0
    )
    place = lax.broadcasted_iota(jnp.int32, (slots, window.shape[0]), 1).astype(F32)
    mine = jnp.where(col_ref[:slots, :1] == place, 1.0, 0.0).astype(F32)
    picked = jnp.dot(mine, window, precision=HIGH, preferred_element_type=F32)
    matrices = picked.T
    square = nproj * nproj
    for n in range(bands):
        energy = col_ref[slots + n : slots + n + 1, :slots]
        mine_n = total[nproj * n : nproj * n + nproj]
        for i in range(nproj):
            at = nproj * i
            mixed = matrices[at : at + nproj] - energy * matrices[square + at : square + at + nproj]
            w_ref[nproj * n + i : nproj * n + i + 1, 0:slots] = jnp.sum(mixed * mine_n, axis=0, keepdims=True)

    lane = lax.broadcasted_iota(jnp.int32, (kinds, slots), 1)
    sub_lo = bf(lax.broadcasted_iota(jnp.int32, (LANES, points), 0))
    sub_hi = bf(lax.broadcasted_iota(jnp.int32, (rows, points), 0))
    zero = jnp.zeros((), BF16)
    one = jnp.ones((), BF16)
    piece = bands * LANES

    def build(s, base):
        idx = idx_ref[pl.ds(s, 1), :]
        lo = bf(idx & 127)
        hi = bf(idx >> 7)
        a_ref[:, base : base + points] = jnp.where(sub_hi == hi, one, zero)
        col = jnp.sum(jnp.where(lane == s, w_ref[:, 0:slots], 0.0), axis=1, keepdims=True)
        v = val_ref[s]
        hit = sub_lo == lo
        for n in range(bands):
            back = jnp.sum(col[nproj * n : nproj * n + nproj] * v, axis=0, keepdims=True)
            big = back.astype(BF16)
            small = (back - big.astype(F32)).astype(BF16)
            at = LANES * n
            b_ref[at : at + LANES, base : base + points] = jnp.where(hit, big, zero)
            b_ref[piece + at : piece + at + LANES, base : base + points] = jnp.where(hit, small, zero)

    acc_ref[...] = jnp.zeros_like(acc_ref)

    def body(c, carry):
        for j in range(chunk):
            build(c * chunk + j, points * j)
        acc_ref[...] += lax.dot_general(
            b_ref[...], a_ref[...], (((1,), (1,)), ((), ())), preferred_element_type=F32
        )
        return carry

    lax.fori_loop(0, steps, body, 0)
    for n in range(bands):
        at = LANES * n
        out_ref[n] = (acc_ref[at : at + LANES] + acc_ref[piece + at : piece + at + LANES]).T


def swapped(value, partner):
    count = lax.axis_size("dom")
    return lax.ppermute(value, "dom", [(s, partner(s) % count) for s in range(count)])


def inner_of(d):
    return d ^ 1


def outer_of(d):
    return d + 1 if d % 2 else d - 1


def across_of(d):
    base, y = d - d % RING, d % RING
    return base + (6, 7, 4, 5, 2, 3, 0, 1)[y]


def beyond_of(d):
    base, y = d - d % RING, d % RING
    if y < HALF:
        return base - RING + (6, 7, 4, 5)[y]
    return base + RING + (2, 3, 0, 1)[y - HALF]


def per_device(
    wave, potential, energies, proj_index, proj_values, slot_atom, atom_rank, d_matrix, q_matrix
):
    bands, planes, ny, nz = wave.shape
    slots, points = proj_index.shape
    nproj = proj_values.shape[1]
    atoms_dev = d_matrix.shape[0]
    kinds = bands * nproj
    rows = planes * ny
    flat = wave.reshape(bands, rows, nz)
    edge = bands * 2 * ny
    height = kinds + 8
    square = nproj * nproj

    def turned(m):
        return jnp.transpose(m, (1, 2, 0)).reshape(square, atoms_dev)

    chunk, aside = 16, 4
    mine, pos, col = pl.pallas_call(
        functools.partial(gather_kernel, chunk, aside),
        out_shape=(
            jax.ShapeDtypeStruct((HALF, height + atoms_dev, LANES), F32),
            jax.ShapeDtypeStruct((slots, LANES), F32),
            jax.ShapeDtypeStruct((slots + 8, LANES), F32),
        ),
        in_specs=[HBM] * 8,
        out_specs=(VMEM, VMEM, VMEM),
        scratch_shapes=[
            pltpu.VMEM((height + atoms_dev, LANES), F32),
            pltpu.SMEM(slot_atom.shape, jnp.int32),
            pltpu.SMEM(atom_rank.shape, jnp.int32),
            pltpu.SMEM(energies.shape, F32),
            pltpu.VMEM(proj_index.shape, jnp.int32),
            pltpu.VMEM(proj_values.shape, F32),
            pltpu.VMEM(flat.shape, F32),
            pltpu.VMEM((square, atoms_dev), F32),
            pltpu.VMEM((square, atoms_dev), F32),
            pltpu.VMEM((bands * rows, 2 * LANES), BF16),
            pltpu.VMEM((2 * LANES, points * (chunk - aside)), BF16),
            pltpu.SemaphoreType.DMA((7 + bands,)),
        ],
        compiler_params=pltpu.CompilerParams(vmem_limit_bytes=40 * MIB),
        cost_estimate=pl.CostEstimate(flops=10**10, bytes_accessed=10**7, transcendentals=0),
        name="gather",
    )(
        *[
            kept(x)
            for x in (
                slot_atom, atom_rank, energies, proj_index, proj_values, flat, turned(d_matrix), turned(q_matrix)
            )
        ]
    )

    count = lax.axis_size("dom")
    groups = [list(range(k, k + HALF)) for k in range(0, count, HALF)]
    got = lax.all_to_all(mine, "dom", 0, 0, axis_index_groups=groups)
    quads = got[:, height:].reshape(HALF * atoms_dev, LANES)
    upper = (lax.axis_index("dom") & 2) == 2
    duo = jnp.where(upper, quads[2 * atoms_dev :], quads[: 2 * atoms_dev])
    half = jnp.concatenate([got[:, :height].sum(0), duo], axis=0)

    inner, outer, base = pl.pallas_call(
        pack_kernel,
        out_shape=(jax.ShapeDtypeStruct((edge, nz), F32),) * 2 + (jax.ShapeDtypeStruct(wave.shape, F32),),
        in_specs=[HBM, HBM, VMEM],
        out_specs=(VMEM, VMEM, VMEM),
        scratch_shapes=[
            pltpu.VMEM(wave.shape, F32),
            pltpu.VMEM(potential.shape, F32),
            pltpu.SemaphoreType.DMA((bands + 1,)),
            pltpu.SemaphoreType.DMA((2, bands, planes // 2)),
        ],
        compiler_params=pltpu.CompilerParams(vmem_limit_bytes=8 * MIB),
        cost_estimate=pl.CostEstimate(flops=10**6, bytes_accessed=10**6, transcendentals=0),
        name="pack",
    )(kept(wave), kept(potential), col)
    beyond = swapped(half, beyond_of)
    across = swapped(half, across_of)
    outer_got = swapped(outer, outer_of)
    inner_got = swapped(inner, inner_of)

    chunk = 16
    added = pl.pallas_call(
        functools.partial(scatter_kernel, chunk),
        out_shape=jax.ShapeDtypeStruct((bands, rows, nz), F32),
        in_specs=[VMEM] * 8,
        out_specs=VMEM,
        scratch_shapes=[
            pltpu.VMEM((rows, points * chunk), BF16),
            pltpu.VMEM((2 * bands * LANES, points * chunk), BF16),
            pltpu.VMEM((2 * bands * LANES, rows), F32),
            pltpu.VMEM((kinds, LANES), F32),
        ],
        compiler_params=pltpu.CompilerParams(vmem_limit_bytes=40 * MIB),
        cost_estimate=pl.CostEstimate(flops=10**10, bytes_accessed=10**7, transcendentals=0),
        name="scatter",
    )(half, quads, across, beyond, pos, col, proj_index, proj_values)

    return pl.pallas_call(
        finish_kernel,
        out_shape=jax.ShapeDtypeStruct(wave.shape, F32),
        in_specs=[VMEM] * 4,
        out_specs=HBM,
        scratch_shapes=[pltpu.VMEM(wave.shape, F32), pltpu.SemaphoreType.DMA((bands,))],
        compiler_params=pltpu.CompilerParams(vmem_limit_bytes=8 * MIB),
        name="finish",
    )(inner_got, outer_got, base, added)


def solution(mesh):
    placed = (
        P("band", "dom", None, None),
        P("dom", None, None),
        P("band"),
        P("dom", None),
        P("dom", None, None),
        P("dom"),
        P(),
        P("dom", None, None),
        P("dom", None, None),
    )
    return jax.shard_map(
        per_device,
        mesh=mesh,
        in_specs=placed,
        out_specs=P("band", "dom", None, None),
        check_vma=False,
    )
```

```python
import functools

import jax
import jax.numpy as jnp
from jax import lax
from jax.experimental import pallas as pl
from jax.experimental.pallas import tpu as pltpu
from jax.sharding import PartitionSpec as P


HIGH = lax.Precision.HIGHEST
F32 = jnp.float32
BF16 = jnp.bfloat16
VMEM = pl.BlockSpec(memory_space=pltpu.VMEM)
HBM = pl.BlockSpec(memory_space=pltpu.HBM)
LANES = 128
HALF = 4
RING = 8
MIB = 1 << 20


def kept(x):
    return pltpu.with_memory_space_constraint(x, pltpu.HBM)


def bf(x):
    return x.astype(F32).astype(BF16)


def pack_kernel(wave_hbm, pot_hbm, col_ref, inner_ref, outer_ref, base_ref, wave_ref, pot_ref, sems, edge_sems):
    bands, planes, ny, nz = wave_ref.shape
    half = planes // 2
    whole = [pltpu.make_async_copy(pot_hbm, pot_ref, sems.at[bands])]
    whole += [pltpu.make_async_copy(wave_hbm.at[n], wave_ref.at[n], sems.at[n]) for n in range(bands)]
    even = (lax.axis_index("dom") & 1) == 0
    edges = []
    for index, (ref, upper) in enumerate(((inner_ref, even), (outer_ref, jnp.logical_not(even)))):
        start = jnp.where(upper, half, 0)
        for n in range(bands):
            for p in range(half):
                edges.append(
                    pltpu.make_async_copy(
                        wave_hbm.at[n, start + p],
                        ref.at[pl.ds((n * half + p) * ny, ny), :],
                        edge_sems.at[index, n, p],
                    )
                )
    for copy in edges + whole:
        copy.start()
    whole[0].wait()
    slots = col_ref.shape[0] - 8
    for n in range(bands):
        whole[1 + n].wait()
        energy = col_ref[slots + n : slots + n + 1, :]
        for x in range(planes):
            f = wave_ref[n, x]
            near = pltpu.roll(f, 1, 0) + pltpu.roll(f, ny - 1, 0)
            near += pltpu.roll(f, 1, 1) + pltpu.roll(f, nz - 1, 1)
            far = pltpu.roll(f, 2, 0) + pltpu.roll(f, ny - 2, 0)
            far += pltpu.roll(f, 2, 1) + pltpu.roll(f, nz - 2, 1)
            for step in (-1, 1):
                if 0 <= x + step < planes:
                    near += wave_ref[n, x + step]
                if 0 <= x + 2 * step < planes:
                    far += wave_ref[n, x + 2 * step]
            base_ref[n, x] = (pot_ref[x] + (3.75 - energy)) * f - (2.0 / 3.0) * near + (1.0 / 24.0) * far
    for copy in edges:
        copy.wait()


def gather_kernel(
    chunk, aside, n_dom, slot_hbm, rank_hbm, energy_hbm, idx_hbm, val_hbm, wave_hbm, d_hbm, q_hbm,
    many_ref, pos_ref, col_ref,
    out_ref, slot_ref, rank_ref, energy_ref, idx_ref, val_ref, wave_ref, d_ref, q_ref, grid_ref, hot_ref, sems
):
    slots, points = idx_ref.shape
    nproj = val_ref.shape[1]
    bands, rows, _ = wave_ref.shape
    atoms_all = rank_ref.shape[0]
    atoms_dev = d_ref.shape[1]
    kinds = bands * nproj
    height = kinds + 8
    copies = [pltpu.make_async_copy(idx_hbm, idx_ref, sems.at[0])]
    copies += [pltpu.make_async_copy(wave_hbm.at[n], wave_ref.at[n], sems.at[1 + n]) for n in range(bands)]
    copies.append(pltpu.make_async_copy(val_hbm, val_ref, sems.at[1 + bands]))
    copies.append(pltpu.make_async_copy(d_hbm, d_ref, sems.at[2 + bands]))
    copies.append(pltpu.make_async_copy(q_hbm, q_ref, sems.at[3 + bands]))
    scalars = [
        pltpu.make_async_copy(source, ref, sems.at[4 + bands + k])
        for k, (source, ref) in enumerate(
            ((slot_hbm, slot_ref), (energy_hbm, energy_ref), (rank_hbm, rank_ref))
        )
    ]
    for copy in copies + scalars:
        copy.start()
    halves = [slice(j, j + LANES) for j in range(0, points, LANES)]
    me = lax.axis_index("dom")
    first = (me & (HALF - 1)) * slots
    lane = lax.broadcasted_iota(jnp.int32, (kinds, LANES), 1) - first
    lane_row = lax.broadcasted_iota(jnp.int32, (8, LANES), 1) - first
    out_ref[:height, :] = jnp.zeros((height, LANES), F32)
    pos_ref[...] = jnp.zeros_like(pos_ref)
    col_ref[...] = jnp.full_like(col_ref, -1.0)
    sub_lo = bf(lax.broadcasted_iota(jnp.int32, (LANES, points), 0))
    for copy in copies[2 + bands :]:
        copy.wait()
    matrices = jnp.concatenate([d_ref[...], q_ref[...]], axis=0)
    matrices = jnp.concatenate(
        [matrices, jnp.zeros((matrices.shape[0], LANES - atoms_dev), F32)], axis=1
    )
    out_ref[height:, :] = matrices.T[:atoms_dev]
    for n in range(bands):
        copies[1 + n].wait()
        w = wave_ref[n]
        big = w.astype(BF16)
        grid_ref[rows * n : rows * n + rows, :LANES] = big
        grid_ref[rows * n : rows * n + rows, LANES:] = (w - big.astype(F32)).astype(BF16)
    copies[0].wait()
    copies[1 + bands].wait()
    for copy in scalars:
        copy.wait()
    for n in range(bands):
        col_ref[slots + n : slots + n + 1, :] = jnp.full((1, LANES), energy_ref[n], F32)
    dense = chunk - aside

    def close(s, accs, sub):
        atom = slot_ref[s]
        live = atom < atoms_all
        pos = rank_ref[jnp.minimum(atom, atoms_all - 1)]
        owner = pos // atoms_dev
        apart = (owner + HALF) ^ (me + HALF)
        apart &= n_dom - 1
        block = jnp.where(apart < RING, (owner + HALF) & (RING - 1), RING + (owner & 1))
        column = jnp.where(live, block * atoms_dev + pos - owner * atoms_dev, -1).astype(F32)
        place = jnp.where(live, pos + 1, 0).astype(F32)
        pos_ref[pl.ds(s, 1), :] = jnp.full((1, LANES), place, F32)
        col_ref[pl.ds(s, 1), :] = jnp.full((1, LANES), column, F32)
        out_ref[kinds:height, :] = jnp.where(lane_row == s, place, out_ref[kinds:height, :])
        cols = []
        for n in range(bands):
            total = None
            for acc, h in zip(accs[n], halves, strict=True):
                pick = jnp.take_along_axis(acc, sub[:, h], axis=0, mode="promise_in_bounds")
                prod = pick * val_ref[s, :, h]
                total = prod if total is None else total + prod
            cols.append(jnp.sum(total, axis=1, keepdims=True))
        col = jnp.concatenate(cols, axis=0)
        out_ref[:kinds, :] = jnp.where(lane == s, col, out_ref[:kinds, :])

    def split(s):
        idx = jnp.broadcast_to(idx_ref[pl.ds(s, 1), :], (8, points))
        return idx >> 10, (idx >> 7) & 7, idx & 127

    def body(c, carry):
        @pl.when(slot_ref[c * chunk] < atoms_all)
        def _():
            for j in range(dense):
                idx = idx_ref[pl.ds(c * chunk + j, 1), :]
                hot = jnp.where(sub_lo == bf(idx & 127), jnp.ones((), BF16), jnp.zeros((), BF16))
                hot_ref[:LANES, points * j : points * j + points] = hot
                hot_ref[LANES:, points * j : points * j + points] = hot
            lines = jnp.dot(grid_ref[...], hot_ref[...], preferred_element_type=F32)
            for j in range(dense):
                s = c * chunk + j
                tile, sub, _ = split(s)
                span = slice(points * j, points * j + points)
                accs = []
                for n in range(bands):
                    at = rows * n
                    acc = lines[at : at + 8, span]
                    for k in range(1, rows // 8):
                        acc = jnp.where(tile == k, lines[at + 8 * k : at + 8 * k + 8, span], acc)
                    accs.append([acc[:, h] for h in halves])
                close(s, accs, sub)
            for j in range(dense, chunk):
                s = c * chunk + j
                tile, sub, lo = split(s)
                accs = [[None] * len(halves) for _ in range(bands)]
                for i, h in enumerate(halves):
                    for k in range(rows // 8):
                        hit = tile[:, h] == k
                        for n in range(bands):
                            line = jnp.take_along_axis(
                                wave_ref[n, 8 * k : 8 * k + 8, :], lo[:, h], axis=1, mode="promise_in_bounds"
                            )
                            accs[n][i] = line if k == 0 else jnp.where(hit, line, accs[n][i])
                close(s, accs, sub)

        return carry

    lax.fori_loop(0, slots // chunk, body, 0)
    for k in range(many_ref.shape[0]):
        many_ref[k] = out_ref[...]


def finish_kernel(inner_ref, outer_ref, base_ref, add_ref, out_hbm, out_ref, sems):
    bands, planes, ny, _ = base_ref.shape
    half = planes // 2
    even = (lax.axis_index("dom") & 1) == 0

    def side(lower, n, p):
        at = (n * half + p) * ny
        inner = inner_ref[at : at + ny, :]
        outer = outer_ref[at : at + ny, :]
        return jnp.where(even, outer, inner) if lower else jnp.where(even, inner, outer)

    copies = []
    for n in range(bands):
        halo = {-2: side(True, n, 0), -1: side(True, n, 1), planes: side(False, n, 0), planes + 1: side(False, n, 1)}
        for x in range(planes):
            value = add_ref[n, ny * x : ny * x + ny, :] + base_ref[n, x]
            for step in (-1, 1):
                if x + step in halo:
                    value -= (2.0 / 3.0) * halo[x + step]
                if x + 2 * step in halo:
                    value += (1.0 / 24.0) * halo[x + 2 * step]
            out_ref[n, x] = value
        copy = pltpu.make_async_copy(out_ref.at[n], out_hbm.at[n], sems.at[n])
        copy.start()
        copies.append(copy)
    for copy in copies:
        copy.wait()


def scatter_kernel(
    chunk, own_ref, quads_ref, across_ref, beyond_ref,
    pos_ref, col_ref, idx_ref, val_ref, out_ref, a_ref, b_ref, acc_ref, w_ref
):
    slots, points = idx_ref.shape
    nproj = val_ref.shape[1]
    bands, rows, _ = out_ref.shape
    kinds = bands * nproj
    height = kinds + 8
    steps = jnp.int32(0)
    for c in range(slots // chunk):
        live = jnp.max(pos_ref[c * chunk : c * chunk + 1, :]) > 0
        steps = steps + live.astype(jnp.int32)
    total = None
    for ref in (own_ref, across_ref, beyond_ref):
        same = jnp.where(pos_ref[...] == ref[kinds : kinds + 1, :], 1.0, 0.0).astype(F32)
        part = lax.dot_general(
            ref[:kinds, :], same, (((1,), (1,)), ((), ())), precision=HIGH, preferred_element_type=F32
        )
        total = part if total is None else total + part
    window = jnp.concatenate(
        [quads_ref[...], across_ref[height:, :]], axis=0
    )
    place = lax.broadcasted_iota(jnp.int32, (slots, window.shape[0]), 1).astype(F32)
    mine = jnp.where(col_ref[:slots, :1] == place, 1.0, 0.0).astype(F32)
    picked = jnp.dot(mine, window, precision=HIGH, preferred_element_type=F32)
    matrices = picked.T
    square = nproj * nproj
    for n in range(bands):
        energy = col_ref[slots + n : slots + n + 1, :slots]
        mine_n = total[nproj * n : nproj * n + nproj]
        for i in range(nproj):
            at = nproj * i
            mixed = matrices[at : at + nproj] - energy * matrices[square + at : square + at + nproj]
            w_ref[nproj * n + i : nproj * n + i + 1, 0:slots] = jnp.sum(mixed * mine_n, axis=0, keepdims=True)

    lane = lax.broadcasted_iota(jnp.int32, (kinds, slots), 1)
    sub_lo = bf(lax.broadcasted_iota(jnp.int32, (LANES, points), 0))
    sub_hi = bf(lax.broadcasted_iota(jnp.int32, (rows, points), 0))
    zero = jnp.zeros((), BF16)
    one = jnp.ones((), BF16)
    piece = bands * LANES

    def build(s, base):
        idx = idx_ref[pl.ds(s, 1), :]
        lo = bf(idx & 127)
        hi = bf(idx >> 7)
        a_ref[:, base : base + points] = jnp.where(sub_hi == hi, one, zero)
        col = jnp.sum(jnp.where(lane == s, w_ref[:, 0:slots], 0.0), axis=1, keepdims=True)
        v = val_ref[s]
        hit = sub_lo == lo
        for n in range(bands):
            back = jnp.sum(col[nproj * n : nproj * n + nproj] * v, axis=0, keepdims=True)
            big = back.astype(BF16)
            small = (back - big.astype(F32)).astype(BF16)
            at = LANES * n
            b_ref[at : at + LANES, base : base + points] = jnp.where(hit, big, zero)
            b_ref[piece + at : piece + at + LANES, base : base + points] = jnp.where(hit, small, zero)

    acc_ref[...] = jnp.zeros_like(acc_ref)

    def body(c, carry):
        for j in range(chunk):
            build(c * chunk + j, points * j)
        acc_ref[...] += lax.dot_general(
            b_ref[...], a_ref[...], (((1,), (1,)), ((), ())), preferred_element_type=F32
        )
        return carry

    lax.fori_loop(0, steps, body, 0)
    for n in range(bands):
        at = LANES * n
        out_ref[n] = (acc_ref[at : at + LANES] + acc_ref[piece + at : piece + at + LANES]).T


def swapped(value, partner):
    count = lax.axis_size("dom")
    return lax.ppermute(value, "dom", [(s, partner(s) % count) for s in range(count)])


def inner_of(d):
    return d ^ 1


def outer_of(d):
    return d + 1 if d % 2 else d - 1


def across_of(d):
    base, y = d - d % RING, d % RING
    return base + (6, 7, 4, 5, 2, 3, 0, 1)[y]


def per_device(
    wave, potential, energies, proj_index, proj_values, slot_atom, atom_rank, d_matrix, q_matrix
):
    bands, planes, ny, nz = wave.shape
    slots, points = proj_index.shape
    nproj = proj_values.shape[1]
    atoms_dev = d_matrix.shape[0]
    kinds = bands * nproj
    rows = planes * ny
    flat = wave.reshape(bands, rows, nz)
    edge = bands * 2 * ny
    height = kinds + 8
    square = nproj * nproj

    def turned(m):
        return jnp.transpose(m, (1, 2, 0)).reshape(square, atoms_dev)

    chunk, aside = 16, 4
    mine, pos, col = pl.pallas_call(
        functools.partial(gather_kernel, chunk, aside, lax.axis_size("dom")),
        out_shape=(
            jax.ShapeDtypeStruct((RING, height + atoms_dev, LANES), F32),
            jax.ShapeDtypeStruct((slots, LANES), F32),
            jax.ShapeDtypeStruct((slots + 8, LANES), F32),
        ),
        in_specs=[HBM] * 8,
        out_specs=(VMEM, VMEM, VMEM),
        scratch_shapes=[
            pltpu.VMEM((height + atoms_dev, LANES), F32),
            pltpu.SMEM(slot_atom.shape, jnp.int32),
            pltpu.SMEM(atom_rank.shape, jnp.int32),
            pltpu.SMEM(energies.shape, F32),
            pltpu.VMEM(proj_index.shape, jnp.int32),
            pltpu.VMEM(proj_values.shape, F32),
            pltpu.VMEM(flat.shape, F32),
            pltpu.VMEM((square, atoms_dev), F32),
            pltpu.VMEM((square, atoms_dev), F32),
            pltpu.VMEM((bands * rows, 2 * LANES), BF16),
            pltpu.VMEM((2 * LANES, points * (chunk - aside)), BF16),
            pltpu.SemaphoreType.DMA((7 + bands,)),
        ],
        compiler_params=pltpu.CompilerParams(vmem_limit_bytes=40 * MIB),
        cost_estimate=pl.CostEstimate(flops=10**10, bytes_accessed=10**7, transcendentals=0),
        name="gather",
    )(
        *[
            kept(x)
            for x in (
                slot_atom, atom_rank, energies, proj_index, proj_values, flat, turned(d_matrix), turned(q_matrix)
            )
        ]
    )

    count = lax.axis_size("dom")
    groups = [[(k + HALF + j) % count for j in range(RING)] for k in range(0, count, RING)]
    got = lax.all_to_all(mine, "dom", 0, 0, axis_index_groups=groups)
    quads = got[:, height:].reshape(RING * atoms_dev, LANES)
    seat = (lax.axis_index("dom") + HALF) & (RING - 1)
    duo = lax.dynamic_slice_in_dim(quads, (seat >> 1) * (2 * atoms_dev), 2 * atoms_dev, 0)
    early, late = got[:HALF, :height].sum(0), got[HALF:, :height].sum(0)
    upper = seat < HALF
    half = jnp.concatenate([jnp.where(upper, early, late), duo], axis=0)
    beyond = jnp.where(upper, late, early)

    inner, outer, base = pl.pallas_call(
        pack_kernel,
        out_shape=(jax.ShapeDtypeStruct((edge, nz), F32),) * 2 + (jax.ShapeDtypeStruct(wave.shape, F32),),
        in_specs=[HBM, HBM, VMEM],
        out_specs=(VMEM, VMEM, VMEM),
        scratch_shapes=[
            pltpu.VMEM(wave.shape, F32),
            pltpu.VMEM(potential.shape, F32),
            pltpu.SemaphoreType.DMA((bands + 1,)),
            pltpu.SemaphoreType.DMA((2, bands, planes // 2)),
        ],
        compiler_params=pltpu.CompilerParams(vmem_limit_bytes=8 * MIB),
        cost_estimate=pl.CostEstimate(flops=10**6, bytes_accessed=10**6, transcendentals=0),
        name="pack",
    )(kept(wave), kept(potential), col)
    across = swapped(half, across_of)
    outer_got = swapped(outer, outer_of)
    inner_got = swapped(inner, inner_of)

    chunk = 16
    added = pl.pallas_call(
        functools.partial(scatter_kernel, chunk),
        out_shape=jax.ShapeDtypeStruct((bands, rows, nz), F32),
        in_specs=[VMEM] * 8,
        out_specs=VMEM,
        scratch_shapes=[
            pltpu.VMEM((rows, points * chunk), BF16),
            pltpu.VMEM((2 * bands * LANES, points * chunk), BF16),
            pltpu.VMEM((2 * bands * LANES, rows), F32),
            pltpu.VMEM((kinds, LANES), F32),
        ],
        compiler_params=pltpu.CompilerParams(vmem_limit_bytes=40 * MIB),
        cost_estimate=pl.CostEstimate(flops=10**10, bytes_accessed=10**7, transcendentals=0),
        name="scatter",
    )(half, quads, across, beyond, pos, col, proj_index, proj_values)

    return pl.pallas_call(
        finish_kernel,
        out_shape=jax.ShapeDtypeStruct(wave.shape, F32),
        in_specs=[VMEM] * 4,
        out_specs=HBM,
        scratch_shapes=[pltpu.VMEM(wave.shape, F32), pltpu.SemaphoreType.DMA((bands,))],
        compiler_params=pltpu.CompilerParams(vmem_limit_bytes=8 * MIB),
        name="finish",
    )(inner_got, outer_got, base, added)


def solution(mesh):
    placed = (
        P("band", "dom", None, None),
        P("dom", None, None),
        P("band"),
        P("dom", None),
        P("dom", None, None),
        P("dom"),
        P(),
        P("dom", None, None),
        P("dom", None, None),
    )
    return jax.shard_map(
        per_device,
        mesh=mesh,
        in_specs=placed,
        out_specs=P("band", "dom", None, None),
        check_vma=False,
    )
```
